128 devices in a mesh: seq: 32 (over z, y, core), slide: 4 (over x).
Axes of the slice: x: 4, y: 4, z: 4, core: 2. Of those that a mesh axis runs over, the one named last changes fastest.
Arguments:
- tile_embed: bfloat16 [16384, 1536], P(('seq', 'slide')), may hold values from -6 to 6
- destination: int32 [16384], P(('seq', 'slide')), may hold values from 0 to 16383, as said below
- slide_lengths: int32 [4], replicated, may hold values from 128 to 8192, as said below
- w_inner: bfloat16 [1536, 3072], replicated, may hold values from -0.15625 to 0.15625
- w_gate: bfloat16 [1536, 3072], replicated, may hold values from -0.15625 to 0.15625
- conv_weight: float32 [2, 4, 3072], replicated, may hold values from -2 to 2
- conv_bias: float32 [2, 3072], replicated, may hold values from -2 to 2
- x_project: bfloat16 [2, 3072, 128], replicated, may hold values from -0.109375 to 0.109375
- dt_project: bfloat16 [2, 96, 3072], replicated, may hold values from -0.625 to 0.625
- dt_bias: float32 [2, 3072], replicated, may hold values from -6 to -3.5
- decay: float32 [2, 16, 3072], replicated, may hold values from 0.0024414062 to 32
- skip_gain: float32 [2, 3072], replicated, may hold values from 0.5 to 1.5
Outputs:
- mixed: bfloat16 [16384, 3072], P(('seq', 'slide'))
The draws below stay inside these ranges and needn't reach their ends.
Inputs may be any that keep to these rules, and one draw needn't show every extreme that they name: `destination`: a permutation; the tile in row b of the 128 rows of each encoder device has a packed position from b * 128 to (b + 1) * 128 - 1. `slide_lengths`: each a multiple of 128; they sum to 16384; the longest is exactly 8192.
All inputs are finite; a program needn't handle non-finite values.
Results may differ from the reference program's by a relative error of at most 0.0067.
Values may be sent and summed in bfloat16 or wider, within the bound.
No kernel may reach another device: no remote copies, remote signals or barrier semaphores. Data moves between devices by JAX's collectives and lax.ppermute only.
A program may use at most 320 MiB of HBM per device.

```python
import jax
import jax.numpy as jnp
from jax import lax

D = 1536
E = 3072
N = 16
R_DT = 96
KCONV = 4
ROWS = 128
SHARDS = 128
TILES = 16384
SEQ_CAP = 8192
SLIDES = 4


def draw_destination(key, part):
    keys = jax.random.split(key, ROWS)
    orders = jax.vmap(lambda one_key: jax.random.permutation(one_key, SHARDS))(keys)
    base = (jnp.arange(ROWS, dtype=jnp.int32) * SHARDS)[:, None]
    return (base + orders.astype(jnp.int32)).T.reshape(-1)


def draw_slide_lengths(key, part):
    units = ROWS // 2
    first_key = jax.random.fold_in(key, 11)
    second_key = jax.random.fold_in(key, 23)
    cuts = jnp.sort(jax.random.permutation(first_key, units - 1)[:SLIDES - 2].astype(jnp.int32) + 1)
    edges = jnp.concatenate([jnp.zeros((1,), jnp.int32), cuts, jnp.full((1,), units, jnp.int32)])
    pieces = edges[1:] - edges[:-1]
    longest = jax.random.randint(second_key, (), 0, SLIDES)
    slide_ids = jnp.arange(SLIDES, dtype=jnp.int32)
    others = jnp.clip(slide_ids - (slide_ids > longest).astype(jnp.int32), 0, SLIDES - 2)
    values = jnp.where(slide_ids == longest, units, pieces[others])
    return (values * SHARDS).astype(jnp.int32)


def draw_decay(key, part):
    order_keys = jax.random.split(jax.random.fold_in(key, 31), 2)
    pick_key = jax.random.fold_in(key, 37)
    fast_key = jax.random.fold_in(key, 41)
    slow_key = jax.random.fold_in(key, 43)
    orders = jax.vmap(lambda one_key: jax.random.permutation(one_key, E))(order_keys)
    slow_channel = orders.astype(jnp.int32) < E // 2
    slow_state = jax.random.randint(pick_key, (2, E), 0, N)
    state_ids = jnp.arange(N, dtype=jnp.int32)
    slow_mask = slow_channel[:, None, :] & (state_ids[None, :, None] == slow_state[:, None, :])
    fast_log = jax.random.uniform(fast_key, (2, N, E), jnp.float32, 0.0, jnp.log(32.0))
    slow_log = jax.random.uniform(slow_key, (2, N, E), jnp.float32, jnp.log(20.0 / SEQ_CAP), jnp.log(150.0 / SEQ_CAP))
    return jnp.where(slow_mask, jnp.exp(slow_log), jnp.exp(fast_log)).astype(jnp.float32)


def levels(stream_key, shape, cuts, least, high):
    loudness, own = 1.0, jax.random.fold_in(stream_key, 6)
    for position, parts in cuts:
        steps = jnp.exp(jax.random.uniform(jax.random.fold_in(own, position), (parts,), jnp.float32, least / len(cuts), high / len(cuts)))
        loudness = loudness * jnp.repeat(steps, shape[position] // parts).reshape([-1 if axis == position else 1 for axis in range(len(shape))])
    return loudness


def scatter_about(own_key, extent, deviation, limit, cuts=(), held_as=jnp.bfloat16):
    factor_of = levels(own_key, extent, cuts, -0.22, 0.18) if cuts else 1.0
    result = jax.random.normal(own_key, extent, jnp.float32) * deviation * factor_of
    return jnp.minimum(jnp.maximum(result, -limit), limit).astype(held_as)


def setup_inputs(seed: int = 0) -> dict:
    streams_of = jax.random.split(jax.random.key(seed), 13)
    return {
        "tile_embed": scatter_about(streams_of[0], (TILES, D), 1.0, 6.0, ((0, 128),)),
        "destination": draw_destination(jax.random.fold_in(streams_of[12], 71), 0),
        "slide_lengths": draw_slide_lengths(jax.random.fold_in(streams_of[12], 71), 0),
        "w_inner": scatter_about(streams_of[3], (D, E), D ** -0.5, 0.15625),
        "w_gate": scatter_about(streams_of[4], (D, E), D ** -0.5, 0.15625),
        "conv_weight": scatter_about(streams_of[5], (2, KCONV, E), 0.5, 2.0, (), jnp.float32),
        "conv_bias": scatter_about(streams_of[6], (2, E), 0.5, 2.0, (), jnp.float32),
        "x_project": scatter_about(streams_of[7], (2, E, R_DT + 2 * N), E ** -0.5, 0.109375),
        "dt_project": scatter_about(streams_of[8], (2, R_DT, E), R_DT ** -0.5, 0.625),
        "dt_bias": jnp.clip(jax.random.uniform(streams_of[9], (2, E), jnp.float32, -6.0, -3.5), -6.0, -3.5),
        "decay": draw_decay(jax.random.fold_in(streams_of[12], 71), 0),
        "skip_gain": jnp.clip(jax.random.uniform(streams_of[11], (2, E), jnp.float32, 0.5, 1.5), 0.5, 1.5),
    }


def sweep(step_size, mixed_in, b_rows, c_rows, rates, skip, reverse):
    def row_step(hidden, row_data):
        dt_row, u_row, b_row, c_row = row_data
        hidden = jnp.exp(dt_row[None, :] * rates) * hidden + (dt_row * u_row)[None, :] * b_row[:, None]
        return hidden, jnp.sum(c_row[:, None] * hidden, axis=0)

    start = jnp.zeros(rates.shape, jnp.float32)
    _, outputs = lax.scan(row_step, start, (step_size, mixed_in, b_rows, c_rows), reverse=reverse)
    return outputs + skip[None, :] * mixed_in


def direction(mixed_in, x_proj, dt_proj, bias, rates, skip, reverse):
    rank = dt_proj.shape[0]
    states = rates.shape[0]
    project = jnp.dot(mixed_in, x_proj, preferred_element_type=jnp.float32)
    low = project[:, :rank].astype(jnp.bfloat16)
    b_rows = project[:, rank:rank + states]
    c_rows = project[:, rank + states:]
    step_size = jax.nn.softplus(jnp.dot(low, dt_proj, preferred_element_type=jnp.float32) + bias[None, :])
    return sweep(step_size, mixed_in.astype(jnp.float32), b_rows, c_rows, rates, skip, reverse)


def reference(tile_embed, destination, slide_lengths, w_inner, w_gate, conv_weight, conv_bias, x_project, dt_project, dt_bias, decay, skip_gain):
    tiles = tile_embed.shape[0]
    width = w_inner.shape[1]
    taps = conv_weight.shape[1]
    projected = jnp.dot(tile_embed, w_inner, preferred_element_type=jnp.float32).astype(jnp.bfloat16)
    packed = jnp.zeros((tiles + SEQ_CAP, width), jnp.bfloat16).at[destination].set(projected)
    offsets = (jnp.cumsum(slide_lengths) - slide_lengths).astype(jnp.int32)
    positions = jnp.arange(SEQ_CAP, dtype=jnp.int32)
    results = jnp.zeros((tiles + SEQ_CAP, width), jnp.bfloat16)
    for slide in range(SLIDES):
        start = offsets[slide].astype(jnp.int32)
        valid = (positions < slide_lengths[slide])[:, None]
        window = lax.dynamic_slice_in_dim(packed, start, SEQ_CAP, 0)
        window = jnp.where(valid, window, jnp.zeros_like(window))
        padded = jnp.pad(window, ((taps - 1, taps - 1), (0, 0)))
        forward_sum = conv_bias[0][None, :]
        backward_sum = conv_bias[1][None, :]
        for tap in range(taps):
            forward_sum = forward_sum + conv_weight[0, tap][None, :] * padded[tap:tap + SEQ_CAP].astype(jnp.float32)
            lead = 2 * (taps - 1) - tap
            backward_sum = backward_sum + conv_weight[1, tap][None, :] * padded[lead:lead + SEQ_CAP].astype(jnp.float32)
        u_fwd = jnp.where(valid, jax.nn.silu(forward_sum), 0.0).astype(jnp.bfloat16)
        u_bwd = jnp.where(valid, jax.nn.silu(backward_sum), 0.0).astype(jnp.bfloat16)
        y_fwd = direction(u_fwd, x_project[0], dt_project[0], dt_bias[0], -decay[0], skip_gain[0], False)
        y_bwd = direction(u_bwd, x_project[1], dt_project[1], dt_bias[1], -decay[1], skip_gain[1], True)
        total = (y_fwd + y_bwd).astype(jnp.bfloat16)
        current = lax.dynamic_slice_in_dim(results, start, SEQ_CAP, 0)
        results = lax.dynamic_update_slice_in_dim(results, current + jnp.where(valid, total, jnp.zeros_like(total)), start, 0)
    gathered = results[destination]
    gate = jnp.dot(tile_embed, w_gate, preferred_element_type=jnp.float32)
    return (gathered.astype(jnp.float32) * jax.nn.silu(gate)).astype(jnp.bfloat16)
```

```python
import jax
import jax.numpy as jnp
from jax import lax
from jax.experimental import pallas as pl
from jax.experimental.pallas import tpu as pltpu
from jax.sharding import PartitionSpec as P

AXES = ("seq", "slide")
SUB = 8
LANES = 128
LOG2E = 1.4426950408889634


def row_positions(shape, per_sub):
    lane = lax.broadcasted_iota(jnp.int32, shape, 1)
    return (lane % SUB) * per_sub + lane // SUB


def one_hot(pos, half):
    place = row_positions(pos.shape, pos.shape[1] // SUB)
    odd = lax.broadcasted_iota(jnp.int32, pos.shape, 0) % 2
    hit = (pos.astype(jnp.int32) == place) & (odd == half)
    return hit.astype(jnp.float32).astype(jnp.bfloat16)


def over_rows(left, right):
    return lax.dot_general(
        left, right, (((0,), (0,)), ((), ())), preferred_element_type=jnp.float32
    )


def sort_kernel(arrived, sorted_rows, ahead, behind, places):
    width = sorted_rows.shape[1] // 2
    rows = sorted_rows.shape[0]
    data = arrived[:, :width]
    pos = arrived[:, width:].astype(jnp.float32)
    places[...] = pos
    lane = lax.broadcasted_iota(jnp.int32, pos.shape, 1)
    odd = lax.broadcasted_iota(jnp.int32, pos.shape, 0) % 2
    edge = jnp.where(lane < SUB, lane + rows - 3, lane - SUB)
    edge = jnp.where((lane % SUB < 3) & (lane < 2 * SUB), edge, -1)
    for half in range(2):
        cols = pl.ds(half * width, width)
        sorted_rows[:, cols] = over_rows(one_hot(pos, half), data).astype(jnp.bfloat16)
        hit = (pos.astype(jnp.int32) == edge) & (odd == half)
        ends = over_rows(hit.astype(jnp.float32).astype(jnp.bfloat16), data)
        ahead[:, cols] = ends[:SUB].astype(jnp.bfloat16)
        behind[:, cols] = ends[SUB : 2 * SUB].astype(jnp.bfloat16)


def sublane(shape):
    return lax.broadcasted_iota(jnp.int32, shape, 0)


def shift_sublanes(tile, count, reverse):
    return pltpu.roll(tile, SUB - count if reverse else count, 0)


def in_reach(count, reverse):
    row = sublane((SUB, LANES))
    return row < SUB - count if reverse else row >= count


def tiles_of(array):
    return [array[SUB * t : SUB * t + SUB] for t in range(array.shape[0] // SUB)]


def in_order(count, reverse):
    return list(range(count))[::-1] if reverse else list(range(count))


def spread_columns(target, d, columns, first, count):
    for n in range(count):
        target[d, n] = jnp.broadcast_to(
            columns[:, first + n : first + n + 1], (columns.shape[0], LANES)
        )


def silu(v):
    return v / (1.0 + jnp.exp(-v))


def softplus(v):
    return jnp.maximum(v, 0.0) + jnp.log1p(jnp.exp(-jnp.abs(v)))


def states_kernel(
    flags,
    rows_in,
    before,
    after,
    w_inner,
    conv_weight,
    conv_bias,
    x_project,
    dt_project,
    dt_bias,
    rates,
    u_out,
    proj_out,
    dt_out,
    inner_states,
    payload,
    all_rows,
    extended,
    b_wide,
):
    step = pl.program_id(0)
    tiles = pl.num_programs(0) // 2
    rows = rows_in.shape[0]
    taps = conv_weight.shape[1]
    reach = taps - 1
    width = w_inner.shape[1]
    states = rates.shape[1]
    rank = dt_project.shape[1]
    slots = rows // SUB

    @pl.when(step == 0)
    def _():
        all_rows[:rows] = rows_in[...]
        all_rows[rows : rows + SUB] = before[...]
        all_rows[rows + SUB :] = after[...]
        proj_out[...] = jnp.zeros_like(proj_out)

    @pl.when(step < tiles)
    def _():
        inner = jnp.dot(all_rows[...], w_inner[...], preferred_element_type=jnp.float32)
        inner = inner.astype(jnp.bfloat16).astype(jnp.float32)
        main = inner[:rows]
        prior = inner[rows : rows + SUB] * flags[0].astype(jnp.float32)
        later = inner[rows + SUB :] * flags[1].astype(jnp.float32)
        row = sublane((SUB, width))
        extended[SUB * reach : SUB * reach + rows] = main
        for k in range(reach):
            own = main[rows - SUB * (reach - k) : rows - SUB * (reach - k - 1)]
            extended[SUB * k : SUB * k + SUB] = jnp.where(
                row == 0, prior[k : k + 1], pltpu.roll(own, 1, 0)
            )
            own = main[SUB * k : SUB * k + SUB]
            base = SUB * (reach + slots + k)
            extended[base : base + SUB] = jnp.where(
                row == SUB - 1, later[k : k + 1], pltpu.roll(own, SUB - 1, 0)
            )
        cols = pl.ds(pl.multiple_of(step * width, LANES), width)
        for d in range(2):
            mixed = conv_bias[d : d + 1, :]
            for tap in range(taps):
                base = SUB * (2 * reach - tap if d else tap)
                mixed = mixed + conv_weight[d, tap : tap + 1, :] * extended[base : base + rows]
            u = silu(mixed).astype(jnp.bfloat16)
            u_out[d, :, cols] = u
            proj_out[d] += jnp.dot(u, x_project[d], preferred_element_type=jnp.float32)

    @pl.when(step == tiles)
    def _():
        for d in range(2):
            spread_columns(b_wide, d, proj_out[d], rank, states)

    @pl.when(step >= tiles)
    def _():
        for d in range(2):
            low = proj_out[d][:, :rank].astype(jnp.bfloat16)
            raw = jnp.dot(low, dt_project[d], preferred_element_type=jnp.float32)
            dt_out[d] = softplus(raw + dt_bias[d : d + 1, :])

        def lane_block(block, carry):
            start = pl.multiple_of(block * LANES, LANES)
            here = pl.ds(start, LANES)
            there = pl.ds(pl.multiple_of((step - tiles) * width + start, LANES), LANES)
            for d in range(2):
                reverse = d == 1
                dt = dt_out[d, :, here]
                fed = tiles_of(dt * u_out[d, :, there].astype(jnp.float32))
                dt = tiles_of(dt)
                total = dt[0]
                for t in range(1, slots):
                    total = total + dt[t]
                finals = []
                for n in range(states):
                    rate = rates[d, n : n + 1, here]
                    state = None
                    for t in in_order(slots, reverse):
                        new = fed[t] * b_wide[d, n, SUB * t : SUB * t + SUB]
                        if state is not None:
                            new = jnp.exp2(dt[t] * rate) * state + new
                        state = new
                    keep = jnp.exp2(total * rate)
                    for count in (1, 2, 4):
                        keep = jnp.where(in_reach(count, reverse), keep, 0.0)
                        state = state + keep * shift_sublanes(state, count, reverse)
                        if count < 4:
                            keep = keep * shift_sublanes(keep, count, reverse)
                    inner_states[d, n, :, here] = state
                    finals.append(state[0:1] if reverse else state[SUB - 1 : SUB])
                whole = jnp.sum(total, axis=0, keepdims=True)
                row = sublane((SUB, LANES))
                for n in range(0, states, 2):
                    out = jnp.where(row == 0, finals[n], finals[n + 1])
                    out = jnp.where(row >= 2, whole, out)
                    payload[d, n // 2, 0, :, here] = out[:4].astype(jnp.bfloat16)
            return carry

        lax.fori_loop(0, width // LANES, lane_block, 0)


def relay_kernel(keep, payload, rates, entering):
    blocks = payload.shape[0]
    backward = keep[blocks]

    def block_step(i, state):
        at = jnp.where(backward == 1, blocks - 1 - i, i)
        state = state * keep[at].astype(jnp.float32)
        entering[at] = state.astype(jnp.bfloat16)
        row = payload[at].astype(jnp.float32)
        return jnp.exp2(rates[...] * row[2:3]) * state + row[0:2]

    lax.fori_loop(0, blocks, block_step, jnp.zeros(rates.shape, jnp.float32), unroll=4)


def outputs_kernel(
    entering,
    inner_states,
    dt_in,
    u_in,
    proj,
    rates,
    skip_gain,
    places,
    out,
    b_wide,
    c_wide,
    mixed,
    partial,
):
    half = pl.program_id(1)
    states = rates.shape[1]
    rows = dt_in.shape[1]
    slots = rows // SUB
    rank = proj.shape[2] - 2 * states

    @pl.when((pl.program_id(0) == 0) & (half == 0))
    def _():
        for d in range(2):
            spread_columns(b_wide, d, proj[d], rank, states)
            spread_columns(c_wide, d, proj[d], rank + states, states)

    def lane_block(block, carry):
        here = pl.ds(pl.multiple_of(block * LANES, LANES), LANES)
        sums = None
        for d in range(2):
            reverse = d == 1
            dt = dt_in[d, :, here]
            u = u_in[d, :, here].astype(jnp.float32)
            fed = tiles_of(dt * u)
            dt = tiles_of(dt)
            u = tiles_of(u)
            ahead = dt[0]
            for t in range(1, slots):
                ahead = ahead + dt[t]
            for count in (1, 2, 4):
                moved = shift_sublanes(ahead, count, reverse)
                ahead = ahead + jnp.where(in_reach(count, reverse), moved, 0.0)
            near = in_reach(1, reverse)
            ahead = jnp.where(near, shift_sublanes(ahead, 1, reverse), 0.0)
            gain = skip_gain[d : d + 1, here]
            if sums is None:
                sums = [gain * tile for tile in u]
            else:
                sums = [total + gain * tile for total, tile in zip(sums, u)]
            for n in range(states):
                rate = rates[d, n : n + 1, here]
                pair = entering[d, n // 2, 0, :, here].astype(jnp.float32)
                state = inner_states[d, n, :, here]
                state = jnp.where(near, shift_sublanes(state, 1, reverse), 0.0)
                state = state + jnp.exp2(ahead * rate) * pair[n % 2 : n % 2 + 1]
                for t in in_order(slots, reverse):
                    at = slice(SUB * t, SUB * t + SUB)
                    state = jnp.exp2(dt[t] * rate) * state + fed[t] * b_wide[d, n, at]
                    sums[t] = sums[t] + c_wide[d, n, at] * state
        for t in range(slots):
            mixed[SUB * t : SUB * t + SUB, here] = sums[t]
        return carry

    lax.fori_loop(0, dt_in.shape[2] // LANES, lane_block, 0)
    pick = one_hot(places[...], half)
    placed = jnp.dot(pick, mixed[...].astype(jnp.bfloat16), preferred_element_type=jnp.float32)

    @pl.when(half == 0)
    def _():
        partial[...] = placed

    @pl.when(half == 1)
    def _():
        out[...] = (partial[...] + placed).astype(jnp.bfloat16)


def gate_kernel(returned, gate, out):
    rows = out.shape[0]
    width = returned.shape[1]
    row = lax.broadcasted_iota(jnp.int32, (rows, 2 * rows), 0)
    col = lax.broadcasted_iota(jnp.int32, (rows, 2 * rows), 1)
    for half in range(2):
        pick = (col == 2 * row + half).astype(jnp.float32).astype(jnp.bfloat16)
        total = jnp.dot(pick, returned[...], preferred_element_type=jnp.float32)
        cols = pl.ds(half * width, width)
        out[:, cols] = (total * gate[:, cols]).astype(jnp.bfloat16)


def full(shape):
    return pl.BlockSpec(shape, lambda *_: (0,) * len(shape))


def local(
    tile_embed,
    destination,
    slide_lengths,
    w_inner,
    w_gate,
    conv_weight,
    conv_bias,
    x_project,
    dt_project,
    dt_bias,
    decay,
    skip_gain,
):
    f32, bf16 = jnp.float32, jnp.bfloat16
    shards = lax.axis_size(AXES)
    me = lax.axis_index(AXES)
    rows, model = tile_embed.shape
    width = w_inner.shape[1]
    states = decay.shape[1]
    rank = dt_project.shape[1]
    taps = conv_weight.shape[1]
    tile = 3 * LANES
    groups = width // tile
    owner_states = 2 * groups * states // shards
    state_groups = states // owner_states
    slots = rows // SUB
    limits = pltpu.CompilerParams(vmem_limit_bytes=56 * 1024 * 1024)

    blocks = jnp.arange(shards, dtype=jnp.int32)
    slide = jnp.arange(slide_lengths.shape[0], dtype=jnp.int32)
    ends = jnp.sum(jnp.where(slide[:, None] <= slide[None, :], slide_lengths[:, None], 0), axis=0)
    starts = ends - slide_lengths
    opens = jnp.any(blocks[:, None] * rows == starts[None, :], axis=1)
    closes = jnp.any((blocks[:, None] + 1) * rows == ends[None, :], axis=1)
    mine = blocks == me
    flags = jnp.stack([~jnp.any(opens & mine), ~jnp.any(closes & mine)]).astype(jnp.int32)
    owner_dir = me // (state_groups * groups)
    owner_group = (me // groups) % state_groups
    owner_tile = me % groups
    keep = jnp.where(owner_dir == 1, ~closes, ~opens).astype(jnp.int32)
    keep = jnp.concatenate([keep, jnp.full((SUB,), owner_dir, jnp.int32)])
    rates = decay * (-LOG2E)
    owner_rates = lax.dynamic_slice(
        rates, (owner_dir, owner_group * owner_states, owner_tile * tile), (1, owner_states, tile)
    )[0]

    offset = (destination - blocks * rows).astype(bf16)
    offset = jnp.broadcast_to(offset[:, None, None], (rows, 2, LANES))
    sent = jnp.concatenate([tile_embed.reshape(rows, 2, model // 2), offset], axis=2)
    arrived = lax.all_to_all(sent, AXES, split_axis=0, concat_axis=0, tiled=True)
    arrived = arrived.reshape(2 * rows, model // 2 + LANES)

    gate = jax.nn.silu(jnp.dot(tile_embed, w_gate, preferred_element_type=f32))

    block_rows, ahead, behind, places = pl.pallas_call(
        sort_kernel,
        out_shape=(
            jax.ShapeDtypeStruct((rows, model), bf16),
            jax.ShapeDtypeStruct((SUB, model), bf16),
            jax.ShapeDtypeStruct((SUB, model), bf16),
            jax.ShapeDtypeStruct((2 * rows, LANES), f32),
        ),
        compiler_params=limits,
        name="sort_rows",
    )(arrived)
    before = lax.ppermute(ahead, AXES, [(i, i + 1) for i in range(shards - 1)])
    after = lax.ppermute(behind, AXES, [(i + 1, i) for i in range(shards - 1)])

    def early(*at):
        return lambda i, *_: tuple(jnp.minimum(i, groups - 1) if a else 0 for a in at)

    def late(*at):
        return lambda i, *_: tuple(jnp.maximum(i - groups, 0) if a else 0 for a in at)

    u, proj, dt, inner_states, payload = pl.pallas_call(
        states_kernel,
        out_shape=(
            jax.ShapeDtypeStruct((2, rows, width), bf16),
            jax.ShapeDtypeStruct((2, rows, LANES), f32),
            jax.ShapeDtypeStruct((2, rows, width), f32),
            jax.ShapeDtypeStruct((2, states, SUB, width), f32),
            jax.ShapeDtypeStruct((2, state_groups, groups, 4, tile), bf16),
        ),
        grid_spec=pltpu.PrefetchScalarGridSpec(
            num_scalar_prefetch=1,
            grid=(2 * groups,),
            in_specs=[
                full((rows, model)),
                full((SUB, model)),
                full((SUB, model)),
                pl.BlockSpec((model, tile), early(0, 1)),
                pl.BlockSpec((2, taps, tile), early(0, 0, 1)),
                pl.BlockSpec((2, tile), early(0, 1)),
                pl.BlockSpec((2, tile, LANES), early(0, 1, 0)),
                pl.BlockSpec((2, rank, tile), late(0, 0, 1)),
                pl.BlockSpec((2, tile), late(0, 1)),
                pl.BlockSpec((2, states, tile), late(0, 0, 1)),
            ],
            out_specs=[
                full((2, rows, width)),
                full((2, rows, LANES)),
                pl.BlockSpec((2, rows, tile), late(0, 0, 1)),
                pl.BlockSpec((2, states, SUB, tile), late(0, 0, 0, 1)),
                pl.BlockSpec((2, state_groups, 1, 4, tile), late(0, 0, 1, 0, 0)),
            ],
            scratch_shapes=[
                pltpu.VMEM((rows + 2 * SUB, model), bf16),
                pltpu.VMEM((rows + 2 * SUB * (taps - 1), tile), f32),
                pltpu.VMEM((2, states, rows, LANES), f32),
            ],
        ),
        compiler_params=limits,
        name="block_states",
    )(
        flags, block_rows, before, after, w_inner, conv_weight, conv_bias,
        x_project, dt_project, dt_bias, rates,
    )

    shared = lax.all_to_all(
        payload.reshape(shards, 4, tile), AXES, split_axis=0, concat_axis=0, tiled=True
    )
    entering = pl.pallas_call(
        relay_kernel,
        out_shape=jax.ShapeDtypeStruct((shards, owner_states, tile), bf16),
        grid_spec=pltpu.PrefetchScalarGridSpec(
            num_scalar_prefetch=1,
            grid=(1,),
            in_specs=[full((shards, 4, tile)), full((owner_states, tile))],
            out_specs=full((shards, owner_states, tile)),
        ),
        compiler_params=limits,
        name="relay",
    )(keep, shared, owner_rates)
    entering = lax.all_to_all(entering, AXES, split_axis=0, concat_axis=0, tiled=True)
    entering = entering.reshape(2, state_groups, groups, owner_states, tile)

    pairs = groups // 2
    totals = pl.pallas_call(
        outputs_kernel,
        out_shape=jax.ShapeDtypeStruct((2 * rows, width // 2), bf16),
        grid=(pairs, 2),
        in_specs=[
            pl.BlockSpec((2, state_groups, 1, owner_states, tile), lambda i, k: (0, 0, k * pairs + i, 0, 0)),
            pl.BlockSpec((2, states, SUB, tile), lambda i, k: (0, 0, 0, k * pairs + i)),
            pl.BlockSpec((2, rows, tile), lambda i, k: (0, 0, k * pairs + i)),
            pl.BlockSpec((2, rows, tile), lambda i, k: (0, 0, k * pairs + i)),
            full((2, rows, LANES)),
            pl.BlockSpec((2, states, tile), lambda i, k: (0, 0, k * pairs + i)),
            pl.BlockSpec((2, tile), lambda i, k: (0, k * pairs + i)),
            full((2 * rows, LANES)),
        ],
        out_specs=pl.BlockSpec((2 * rows, tile), lambda i, k: (0, i)),
        scratch_shapes=[
            pltpu.VMEM((2, states, rows, LANES), f32),
            pltpu.VMEM((2, states, rows, LANES), f32),
            pltpu.VMEM((rows, tile), f32),
            pltpu.VMEM((2 * rows, tile), f32),
        ],
        compiler_params=limits,
        name="block_outputs",
    )(entering, inner_states, dt, u, proj, rates, skip_gain, places)

    returned = lax.all_to_all(
        totals.reshape(rows, 2, width // 2), AXES, split_axis=0, concat_axis=0, tiled=True
    )
    return pl.pallas_call(
        gate_kernel,
        out_shape=jax.ShapeDtypeStruct((rows, width), bf16),
        compiler_params=limits,
        name="gated",
    )(returned.reshape(2 * rows, width // 2), gate)


def solution(mesh):
    placed = (P(AXES, None), P(AXES)) + (P(),) * 10
    return jax.shard_map(
        local, mesh=mesh, in_specs=placed, out_specs=P(AXES, None), check_vma=False
    )
```

```python
import functools

import jax
import jax.numpy as jnp
from jax import lax
from jax.experimental import pallas as pl
from jax.experimental.pallas import tpu as pltpu
from jax.sharding import PartitionSpec as P

AXES = ("seq", "slide")
SUB = 8
LANES = 128
LOG2E = 1.4426950408889634


def spread_index(rows, turned=False):
    shape = (rows, rows)
    row = lax.broadcasted_iota(jnp.int32, shape, 1 if turned else 0)
    col = lax.broadcasted_iota(jnp.int32, shape, 0 if turned else 1)
    group = rows // SUB
    hit = (row // SUB == col % group) & (row % SUB == col // group)
    return hit.astype(jnp.float32).astype(jnp.bfloat16)


def as_bf16(product):
    return product.astype(jnp.bfloat16)


def matmul(left, right):
    return jnp.dot(left, right, preferred_element_type=jnp.float32)


def over_rows(left, right):
    return lax.dot_general(
        left, right, (((0,), (0,)), ((), ())), preferred_element_type=jnp.float32
    )


def chunked(pieces, out):
    rows = pieces[0].shape[0]
    group = rows // SUB
    spread = spread_index(rows)
    blank = [jnp.zeros_like(pieces[0])] * (SUB - len(pieces))
    for q in range(SUB):
        part = [piece[group * q : group * q + group] for piece in list(pieces) + blank]
        out[rows * q : rows * q + rows] = as_bf16(matmul(spread, jnp.concatenate(part, axis=0)))


def pack_kernel(embed, destination, out):
    rows = embed.shape[0]
    width = out.shape[1]
    pieces = [embed[:, at : at + width] for at in range(0, embed.shape[1], width)]
    row = lax.broadcasted_iota(jnp.int32, (rows, rows), 0)
    col = lax.broadcasted_iota(jnp.int32, (rows, rows), 1)
    offset = jnp.where(row == col, destination[...] - rows * col, 0)
    offset = as_bf16(offset.astype(jnp.float32))
    pieces.append(as_bf16(matmul(offset, jnp.ones((rows, width), jnp.bfloat16))))
    chunked(pieces, out)


def row_positions(shape, per_sub):
    lane = lax.broadcasted_iota(jnp.int32, shape, 1)
    return (lane % SUB) * per_sub + lane // SUB


def one_hot(pos):
    place = row_positions(pos.shape, pos.shape[1] // SUB)
    hit = pos.astype(jnp.int32) == place
    return hit.astype(jnp.float32).astype(jnp.bfloat16)


def sort_kernel(arrived, sorted_rows, ahead, behind, places, plain):
    rows = sorted_rows.shape[0]
    group = rows // SUB
    width = arrived.shape[1]
    pieces = sorted_rows.shape[1] // width
    gather = spread_index(rows, turned=True)
    for q in range(SUB):
        part = as_bf16(matmul(gather, arrived[rows * q : rows * q + rows]))
        for k in range(pieces + 1):
            plain[group * q : group * q + group, width * k : width * k + width] = part[
                group * k : group * k + group
            ]
    pos = plain[:, width * pieces : width * pieces + LANES].astype(jnp.float32)
    places[...] = pos
    lane = lax.broadcasted_iota(jnp.int32, pos.shape, 1)
    edge = jnp.where(lane < SUB, lane + rows - 3, lane - SUB)
    edge = jnp.where((lane % SUB < 3) & (lane < 2 * SUB), edge, -1)
    hit = (pos.astype(jnp.int32) == edge).astype(jnp.float32).astype(jnp.bfloat16)
    data = plain[:, : width * pieces]
    ends = as_bf16(over_rows(hit, data))
    ahead[...] = ends[:SUB]
    behind[...] = ends[SUB : 2 * SUB]
    sorted_rows[...] = as_bf16(over_rows(one_hot(pos), data))


def inner_kernel(rows_in, weight, x_project, dt_project, out, weight_here, x_here, dt_here, sems):
    parts = sems.shape[0] - 2
    width = weight.shape[1] // parts
    copies = []
    for k in range(parts):
        cols = pl.ds(k * width, width)
        copies.append((weight.at[:, cols], weight_here.at[:, cols]))
    copies += [(x_project, x_here), (dt_project, dt_here)]
    copies = [
        pltpu.make_async_copy(here, there, sems.at[k]) for k, (here, there) in enumerate(copies)
    ]
    for copy in copies:
        copy.start()
    for k in range(parts):
        cols = pl.ds(k * width, width)
        copies[k].wait()
        out[:, cols] = as_bf16(matmul(rows_in[...], weight_here[:, cols]))
    copies[parts].wait()
    copies[parts + 1].wait()


def sublane(shape):
    return lax.broadcasted_iota(jnp.int32, shape, 0)


def shift_sublanes(tile, count, reverse):
    return pltpu.roll(tile, SUB - count if reverse else count, 0)


def in_reach(count, reverse):
    row = sublane((SUB, LANES))
    return row < SUB - count if reverse else row >= count


def outside(total, reverse):
    for count in (1, 2, 4):
        moved = shift_sublanes(total, count, reverse)
        total = total + jnp.where(in_reach(count, reverse), moved, 0.0)
    return jnp.where(in_reach(1, reverse), shift_sublanes(total, 1, reverse), 0.0)


def tiles_of(array):
    return [array[SUB * t : SUB * t + SUB] for t in range(array.shape[0] // SUB)]


def in_order(count, reverse):
    return list(range(count))[::-1] if reverse else list(range(count))


def spread_columns(target, columns, first, count):
    for n in range(count):
        target[n] = jnp.broadcast_to(
            columns[:, first + n : first + n + 1], (columns.shape[0], LANES)
        )


def silu(v):
    return v / (1.0 + jnp.exp(-v))


def softplus(v):
    return jnp.maximum(v, 0.0) + jnp.log(1.0 + jnp.exp(-jnp.abs(v)))


def states_kernel(
    flags,
    inner_in,
    before,
    after,
    w_inner,
    conv_weight,
    conv_bias,
    x_project,
    dt_project,
    dt_bias,
    rates,
    u_result,
    proj_result,
    dt_result,
    payload_result,
    u_out,
    proj_out,
    dt_out,
    b_wide,
    payload,
    edge_rows,
    extended,
    sems,
):
    copies = [
        pltpu.make_async_copy(here, there, sems.at[k])
        for k, (here, there) in enumerate(
            (
                (u_out, u_result),
                (proj_out, proj_result),
                (dt_out, dt_result),
                (payload.at[0], payload_result.at[0]),
                (payload.at[1], payload_result.at[1]),
            )
        )
    ]
    rows, channels = inner_in.shape
    taps = conv_weight.shape[1]
    reach = taps - 1
    width = extended.shape[1]
    states = rates.shape[1]
    rank = dt_project.shape[1]
    slots = rows // SUB
    tile = payload.shape[4]
    edge_rows[:SUB] = before[...]
    edge_rows[SUB:] = after[...]
    proj_out[...] = jnp.zeros_like(proj_out)

    def conv_block(step, carry):
        cols = pl.ds(pl.multiple_of(step * width, LANES), width)
        edges = as_bf16(matmul(edge_rows[...], w_inner[:, cols])).astype(jnp.float32)
        main = inner_in[:, cols].astype(jnp.float32)
        prior = edges[:SUB] * flags[0].astype(jnp.float32)
        later = edges[SUB:] * flags[1].astype(jnp.float32)
        row = sublane((SUB, width))
        extended[SUB * reach : SUB * reach + rows] = main
        for k in range(reach):
            own = main[rows - SUB * (reach - k) : rows - SUB * (reach - k - 1)]
            extended[SUB * k : SUB * k + SUB] = jnp.where(
                row == 0, prior[k : k + 1], pltpu.roll(own, 1, 0)
            )
            own = main[SUB * k : SUB * k + SUB]
            base = SUB * (reach + slots + k)
            extended[base : base + SUB] = jnp.where(
                row == SUB - 1, later[k : k + 1], pltpu.roll(own, SUB - 1, 0)
            )
        for d in range(2):
            mixed = conv_bias[d : d + 1, cols]
            for tap in range(taps):
                base = SUB * (2 * reach - tap if d else tap)
                gain = conv_weight[d, tap : tap + 1, cols]
                mixed = mixed + gain * extended[base : base + rows]
            u = as_bf16(silu(mixed))
            u_out[d, :, cols] = u
            proj_out[d] += matmul(u, x_project[d, cols, :])
        return carry

    lax.fori_loop(0, channels // width, conv_block, 0)
    copies[0].start()
    copies[1].start()
    for d in range(2):
        spread_columns(b_wide.at[d], proj_out[d], rank, states)

    def step_block(step, carry):
        cols = pl.ds(pl.multiple_of(step * width, LANES), width)
        for d in range(2):
            low = as_bf16(proj_out[d][:, :rank])
            raw = matmul(low, dt_project[d, :, cols])
            dt_out[d, :, cols] = softplus(raw + dt_bias[d : d + 1, cols])
        return carry

    lax.fori_loop(0, channels // width, step_block, 0)
    copies[2].start()
    row = sublane((SUB, LANES))

    def state_block(block, carry, d):
        here = pl.ds(pl.multiple_of(block * LANES, LANES), LANES)
        group = block // (tile // LANES)
        within = pl.multiple_of((block - group * (tile // LANES)) * LANES, LANES)
        reverse = d == 1
        dt = dt_out[d, :, here]
        fed = tiles_of(dt * u_out[d, :, here].astype(jnp.float32))
        dt = tiles_of(dt)
        order = in_order(slots, not reverse)
        rest = {order[0]: None}
        total = dt[order[0]]
        for t in order[1:]:
            rest[t] = total
            total = total + dt[t]
        outer = outside(total, not reverse)
        whole = total + outer
        whole = whole[SUB - 1 : SUB] if reverse else whole[0:1]
        rest = {t: outer if part is None else part + outer for t, part in rest.items()}
        finals = []
        for n in range(states):
            rate = rates[d, n : n + 1, here]
            state = None
            for t in order:
                new = fed[t] * b_wide[d, n, SUB * t : SUB * t + SUB]
                new = jnp.exp2(rest[t] * rate) * new
                state = new if state is None else state + new
            finals.append(jnp.sum(state, axis=0, keepdims=True))
        for n in range(0, states, 2):
            out = jnp.where(row == 0, finals[n], finals[n + 1])
            out = jnp.where(row >= 2, whole, out)
            payload[d, n // 2, group, :, pl.ds(within, LANES)] = as_bf16(out[:4])
        return carry

    for d in range(2):
        lax.fori_loop(0, channels // LANES, functools.partial(state_block, d=d), 0)
        copies[3 + d].start()
    for copy in copies:
        copy.wait()


def local_kernel(dt_in, u_in, proj, rates, skip_gain, y_out, entry_out, b_wide, c_wide, *, reverse):
    d = int(reverse)
    states = rates.shape[1]
    rows, channels = y_out.shape
    slots = rows // SUB
    rank = proj.shape[2] - 2 * states

    @pl.when(pl.program_id(0) == 0)
    def _():
        spread_columns(b_wide, proj[0], rank, states)
        spread_columns(c_wide, proj[0], rank + states, states)

    def lane_block(block, carry):
        here = pl.ds(pl.multiple_of(block * LANES, LANES), LANES)
        dt = dt_in[0, :, here]
        u = u_in[0, :, here].astype(jnp.float32)
        fed = tiles_of(dt * u)
        dt = tiles_of(dt)
        gain = skip_gain[d : d + 1, here]
        sums = [gain * tile for tile in tiles_of(u)]
        total = dt[0]
        for t in range(1, slots):
            total = total + dt[t]
        for n in range(states):
            rate = rates[0, n : n + 1, here]
            state = None
            for t in in_order(slots, reverse):
                at = slice(SUB * t, SUB * t + SUB)
                new = fed[t] * b_wide[n, at]
                if state is not None:
                    new = jnp.exp2(dt[t] * rate) * state + new
                state = new
                sums[t] = sums[t] + c_wide[n, at] * state
            keep = jnp.exp2(total * rate)
            for count in (1, 2, 4):
                keep = jnp.where(in_reach(count, reverse), keep, 0.0)
                state = state + keep * shift_sublanes(state, count, reverse)
                if count < 4:
                    keep = keep * shift_sublanes(keep, count, reverse)
            near = in_reach(1, reverse)
            entry_out[n, :, here] = jnp.where(near, shift_sublanes(state, 1, reverse), 0.0)
        for t in range(slots):
            y_out[SUB * t : SUB * t + SUB, here] = sums[t]
        return carry

    lax.fori_loop(0, channels // LANES, lane_block, 0)


def relay_kernel(keep, payload, rates, entering):
    blocks = payload.shape[0]
    backward = keep[blocks]

    def block_step(i, state):
        at = jnp.where(backward == 1, blocks - 1 - i, i)
        state = state * keep[at].astype(jnp.float32)
        entering[at] = state.astype(jnp.bfloat16)
        row = payload[at].astype(jnp.float32)
        return jnp.exp2(rates[...] * row[2:3]) * state + row[0:2]

    lax.fori_loop(0, blocks, block_step, jnp.zeros(rates.shape, jnp.float32), unroll=16)


def outputs_kernel(
    entering,
    entry_fwd,
    entry_bwd,
    y_fwd,
    y_bwd,
    dt_in,
    proj,
    rates,
    places,
    out,
    c_wide,
    mixed,
    placed,
):
    step = pl.program_id(0)
    states = rates.shape[1]
    rows, channels = y_fwd.shape
    slots = rows // SUB
    rank = proj.shape[2] - 2 * states

    @pl.when(step == 0)
    def _():
        for d in range(2):
            spread_columns(c_wide.at[d], proj[d], rank + states, states)

    def lane_block(block, carry, d, entry):
        here = pl.ds(pl.multiple_of(block * LANES, LANES), LANES)
        reverse = d == 1
        sums = tiles_of(mixed[:, here] if reverse else y_fwd[:, here] + y_bwd[:, here])
        dt = tiles_of(dt_in[d, :, here])
        order = in_order(slots, reverse)
        past = {}
        total = None
        for t in order:
            total = dt[t] if total is None else total + dt[t]
            past[t] = total
        ahead = outside(total, reverse)
        for n in range(states):
            rate = rates[d, n : n + 1, here]
            pair = entering[d, n // 2, 0, :, here].astype(jnp.float32)
            state = jnp.exp2(ahead * rate) * pair[n % 2 : n % 2 + 1] + entry[n, :, here]
            for t in order:
                at = slice(SUB * t, SUB * t + SUB)
                decayed = jnp.exp2(past[t] * rate)
                sums[t] = sums[t] + decayed * (c_wide[d, n, at] * state)
        for t in range(slots):
            mixed[SUB * t : SUB * t + SUB, here] = sums[t]
        return carry

    for d, entry in ((0, entry_fwd), (1, entry_bwd)):
        lax.fori_loop(0, channels // LANES, functools.partial(lane_block, d=d, entry=entry), 0)
    placed[step] = as_bf16(matmul(one_hot(places[...]), as_bf16(mixed[...])))

    @pl.when(step == pl.num_programs(0) - 1)
    def _():
        chunked([placed[k] for k in range(SUB)], out)


def gate_kernel(returned, gate, out):
    rows = out.shape[0]
    group = rows // SUB
    width = returned.shape[1]
    gather = spread_index(rows, turned=True)
    for q in range(SUB):
        part = matmul(gather, returned[rows * q : rows * q + rows])
        here = slice(group * q, group * q + group)
        for k in range(SUB):
            cols = slice(width * k, width * k + width)
            out[here, cols] = as_bf16(part[group * k : group * k + group] * gate[here, cols])


def limits(mebibytes):
    return pltpu.CompilerParams(vmem_limit_bytes=mebibytes * 1024 * 1024)


def in_vmem(array):
    return pltpu.with_memory_space_constraint(array, pltpu.VMEM)


def in_hbm(array):
    return pltpu.with_memory_space_constraint(array, pltpu.HBM)


def on_chip(kernel, name, mebibytes, results, *operands, scalars=0, scratch=()):
    places = [pltpu.SMEM] * scalars + [pltpu.VMEM] * (len(operands) - scalars)
    one = pl.BlockSpec(memory_space=pltpu.VMEM)
    return pl.pallas_call(
        kernel,
        out_shape=results,
        in_specs=[pl.BlockSpec(memory_space=place) for place in places],
        out_specs=tuple(one for _ in results) if isinstance(results, tuple) else one,
        scratch_shapes=list(scratch),
        compiler_params=limits(mebibytes),
        name=name,
    )(
        *(
            in_vmem(operand) if place is pltpu.VMEM else operand
            for operand, place in zip(operands, places)
        )
    )


def local(
    tile_embed,
    destination,
    slide_lengths,
    w_inner,
    w_gate,
    conv_weight,
    conv_bias,
    x_project,
    dt_project,
    dt_bias,
    decay,
    skip_gain,
):
    f32, bf16 = jnp.float32, jnp.bfloat16
    shards = lax.axis_size(AXES)
    me = lax.axis_index(AXES)
    rows, model = tile_embed.shape
    width = w_inner.shape[1]
    states = decay.shape[1]
    rank = dt_project.shape[1]
    taps = conv_weight.shape[1]
    tile = 3 * LANES
    groups = width // tile
    owner_states = 2 * groups * states // shards
    state_groups = states // owner_states
    slots = rows // SUB

    blocks = jnp.arange(shards, dtype=jnp.int32)
    slide = jnp.arange(slide_lengths.shape[0], dtype=jnp.int32)
    ends = jnp.sum(jnp.where(slide[:, None] <= slide[None, :], slide_lengths[:, None], 0), axis=0)
    starts = ends - slide_lengths
    opens = jnp.any(blocks[:, None] * rows == starts[None, :], axis=1)
    closes = jnp.any((blocks[:, None] + 1) * rows == ends[None, :], axis=1)
    mine = blocks == me
    flags = jnp.stack([~jnp.any(opens & mine), ~jnp.any(closes & mine)]).astype(jnp.int32)
    owner_dir = me // (state_groups * groups)
    owner_group = (me // groups) % state_groups
    owner_tile = me % groups
    keep = jnp.where(owner_dir == 1, ~closes, ~opens).astype(jnp.int32)
    keep = jnp.concatenate([keep, jnp.full((SUB,), owner_dir, jnp.int32)])
    rates = decay * (-LOG2E)
    owner_rates = lax.dynamic_slice(
        rates, (owner_dir, owner_group * owner_states, owner_tile * tile), (1, owner_states, tile)
    )[0]

    piece = 2 * LANES
    sent = on_chip(
        pack_kernel, "pack", 3, pltpu.VMEM((SUB * rows, piece), bf16), tile_embed, destination[None, :]
    )
    arrived = lax.all_to_all(
        sent.reshape(rows, SUB, piece), AXES, split_axis=0, concat_axis=0, tiled=True
    ).reshape(SUB * rows, piece)
    gate = jax.nn.silu(jnp.dot(tile_embed, w_gate, preferred_element_type=f32))

    block_rows, ahead, behind, places = on_chip(
        sort_kernel,
        "sort_rows",
        4,
        (
            pltpu.VMEM((rows, model), bf16),
            pltpu.VMEM((SUB, model), bf16),
            pltpu.VMEM((SUB, model), bf16),
            pltpu.HBM((rows, LANES), f32),
        ),
        arrived,
        scratch=[pltpu.VMEM((rows, model + piece), bf16)],
    )
    before = lax.ppermute(ahead, AXES, [(i, i + 1) for i in range(shards - 1)])
    after = lax.ppermute(behind, AXES, [(i + 1, i) for i in range(shards - 1)])
    hbm_spec = pl.BlockSpec(memory_space=pltpu.HBM)
    vmem_spec = pl.BlockSpec(memory_space=pltpu.VMEM)
    weights = (w_inner, x_project, dt_project)
    inner, w_inner, x_project, dt_project = pl.pallas_call(
        inner_kernel,
        out_shape=(
            pltpu.VMEM((rows, width), bf16),
            *(pltpu.VMEM(w.shape, w.dtype) for w in weights),
        ),
        in_specs=[vmem_spec] + [hbm_spec] * 3,
        out_specs=(vmem_spec,) * 4,
        scratch_shapes=[pltpu.SemaphoreType.DMA((6,))],
        compiler_params=limits(2),
        name="inner",
    )(in_vmem(block_rows), *(in_hbm(w) for w in weights))

    operands = (
        inner, before, after, w_inner, conv_weight, conv_bias, x_project, dt_project, dt_bias, rates,
    )
    on_chip_results = [
        pltpu.VMEM((2, rows, width), bf16),
        pltpu.VMEM((2, rows, LANES), f32),
        pltpu.VMEM((2, rows, width), f32),
        pltpu.VMEM((2, states, rows, LANES), f32),
        pltpu.VMEM((2, state_groups, groups, 4, tile), bf16),
    ]
    u, proj, dt, payload = pl.pallas_call(
        states_kernel,
        out_shape=(
            pltpu.HBM((2, rows, width), bf16),
            pltpu.HBM((2, rows, LANES), f32),
            pltpu.HBM((2, rows, width), f32),
            pltpu.HBM((2, state_groups, groups, 4, tile), bf16),
        ),
        in_specs=[pl.BlockSpec(memory_space=pltpu.SMEM)] + [vmem_spec] * len(operands),
        out_specs=(hbm_spec,) * 4,
        scratch_shapes=on_chip_results
        + [
            pltpu.VMEM((2 * SUB, model), bf16),
            pltpu.VMEM((rows + 2 * SUB * (taps - 1), 2 * tile), f32),
            pltpu.SemaphoreType.DMA((5,)),
        ],
        compiler_params=limits(14),
        name="block_states",
    )(flags, *(in_vmem(operand) for operand in operands))

    def local_outputs(d):
        return pl.pallas_call(
            functools.partial(local_kernel, reverse=d == 1),
            out_shape=(
                pltpu.HBM((rows, width), f32),
                pltpu.HBM((states, SUB, width), f32),
            ),
            grid=(groups,),
            in_specs=[
                pl.BlockSpec((1, rows, tile), lambda i: (d, 0, i)),
                pl.BlockSpec((1, rows, tile), lambda i: (d, 0, i)),
                pl.BlockSpec((1, rows, LANES), lambda i: (d, 0, 0)),
                pl.BlockSpec((1, states, tile), lambda i: (d, 0, i)),
                pl.BlockSpec((2, tile), lambda i: (0, i)),
            ],
            out_specs=[
                pl.BlockSpec((rows, tile), lambda i: (0, i)),
                pl.BlockSpec((states, SUB, tile), lambda i: (0, 0, i)),
            ],
            scratch_shapes=[pltpu.VMEM((states, rows, LANES), f32)] * 2,
            compiler_params=limits(6),
            name="local_bwd_outputs" if d else "local_fwd_outputs",
        )(in_hbm(dt), in_hbm(u), in_hbm(proj), rates, skip_gain)

    local_fwd = local_outputs(0)
    local_bwd = local_outputs(1)

    shared = lax.all_to_all(
        payload.reshape(shards, 4, tile), AXES, split_axis=0, concat_axis=0, tiled=True
    )
    shared, *local_fwd = lax.optimization_barrier((shared, *local_fwd))
    entering = on_chip(
        relay_kernel,
        "relay",
        2,
        pltpu.VMEM((shards, owner_states, tile), bf16),
        keep, shared, owner_rates,
        scalars=1,
    )
    entering = lax.all_to_all(entering, AXES, split_axis=0, concat_axis=0, tiled=True)
    entering, *local_bwd = lax.optimization_barrier((entering, *local_bwd))
    entering = entering.reshape(2, state_groups, groups, owner_states, tile)
    y_fwd, entry_fwd = local_fwd
    y_bwd, entry_bwd = local_bwd

    totals = pl.pallas_call(
        outputs_kernel,
        out_shape=pltpu.HBM((SUB * rows, tile), bf16),
        grid=(groups,),
        in_specs=[
            pl.BlockSpec((2, state_groups, 1, owner_states, tile), lambda i: (0, 0, i, 0, 0)),
            pl.BlockSpec((states, SUB, tile), lambda i: (0, 0, i)),
            pl.BlockSpec((states, SUB, tile), lambda i: (0, 0, i)),
            pl.BlockSpec((rows, tile), lambda i: (0, i)),
            pl.BlockSpec((rows, tile), lambda i: (0, i)),
            pl.BlockSpec((2, rows, tile), lambda i: (0, 0, i)),
            pl.BlockSpec((2, rows, LANES), lambda i: (0, 0, 0)),
            pl.BlockSpec((2, states, tile), lambda i: (0, 0, i)),
            pl.BlockSpec((rows, LANES), lambda i: (0, 0)),
        ],
        out_specs=pl.BlockSpec((SUB * rows, tile), lambda i: (0, 0)),
        scratch_shapes=[
            pltpu.VMEM((2, states, rows, LANES), f32),
            pltpu.VMEM((rows, tile), f32),
            pltpu.VMEM((groups, rows, tile), bf16),
        ],
        compiler_params=limits(12),
        name="block_outputs",
    )(
        in_vmem(entering),
        *(in_hbm(array) for array in (entry_fwd, entry_bwd, y_fwd, y_bwd, dt, proj)),
        rates,
        in_hbm(places),
    )

    returned = lax.all_to_all(
        totals.reshape(rows, SUB, tile), AXES, split_axis=0, concat_axis=0, tiled=True
    ).reshape(SUB * rows, tile)
    return pl.pallas_call(
        gate_kernel,
        out_shape=jax.ShapeDtypeStruct((rows, width), bf16),
        compiler_params=limits(5),
        name="gated",
    )(in_vmem(returned), gate)


def solution(mesh):
    placed = (P(AXES, None), P(AXES)) + (P(),) * 10
    return jax.shard_map(
        local, mesh=mesh, in_specs=placed, out_specs=P(AXES, None), check_vma=False
    )
```

```python
import functools

import jax
import jax.numpy as jnp
from jax import lax
from jax.experimental import pallas as pl
from jax.experimental.pallas import tpu as pltpu
from jax.sharding import PartitionSpec as P

AXES = ("seq", "slide")
SUB = 8
LANES = 128
PACK = 16
LOG2E = 1.4426950408889634


def spread_index(rows, turned=False):
    shape = (rows, rows)
    row = lax.broadcasted_iota(jnp.int32, shape, 1 if turned else 0)
    col = lax.broadcasted_iota(jnp.int32, shape, 0 if turned else 1)
    group = rows // SUB
    hit = (row // SUB == col % group) & (row % SUB == col // group)
    return hit.astype(jnp.float32).astype(jnp.bfloat16)


def as_bf16(product):
    return product.astype(jnp.bfloat16)


def matmul(left, right):
    return jnp.dot(left, right, preferred_element_type=jnp.float32)


def over_rows(left, right):
    return lax.dot_general(
        left, right, (((0,), (0,)), ((), ())), preferred_element_type=jnp.float32
    )


def chunked(pieces, out):
    rows = pieces[0].shape[0]
    group = rows // SUB
    spread = spread_index(rows)
    blank = [jnp.zeros_like(pieces[0])] * (SUB - len(pieces))
    for q in range(SUB):
        part = [piece[group * q : group * q + group] for piece in list(pieces) + blank]
        out[rows * q : rows * q + rows] = as_bf16(matmul(spread, jnp.concatenate(part, axis=0)))


def pack_kernel(embed, destination, out):
    rows = embed.shape[0]
    width = out.shape[1]
    pieces = [embed[:, at : at + width] for at in range(0, embed.shape[1], width)]
    row = lax.broadcasted_iota(jnp.int32, (rows, rows), 0)
    col = lax.broadcasted_iota(jnp.int32, (rows, rows), 1)
    offset = jnp.where(row == col, destination[...] - rows * col, 0)
    offset = as_bf16(offset.astype(jnp.float32))
    pieces.append(as_bf16(matmul(offset, jnp.ones((rows, width), jnp.bfloat16))))
    chunked(pieces, out)


def row_positions(shape, per_sub):
    lane = lax.broadcasted_iota(jnp.int32, shape, 1)
    return (lane % SUB) * per_sub + lane // SUB


def one_hot(pos):
    place = row_positions(pos.shape, pos.shape[1] // SUB)
    hit = pos.astype(jnp.int32) == place
    return hit.astype(jnp.float32).astype(jnp.bfloat16)


def sort_kernel(arrived, sorted_rows, ahead, behind, places, plain):
    rows = sorted_rows.shape[0]
    group = rows // SUB
    width = arrived.shape[1]
    pieces = sorted_rows.shape[1] // width
    gather = spread_index(rows, turned=True)
    for q in range(SUB):
        part = as_bf16(matmul(gather, arrived[rows * q : rows * q + rows]))
        for k in range(pieces + 1):
            plain[group * q : group * q + group, width * k : width * k + width] = part[
                group * k : group * k + group
            ]
    pos = plain[:, width * pieces : width * pieces + LANES].astype(jnp.float32)
    places[...] = pos
    lane = lax.broadcasted_iota(jnp.int32, pos.shape, 1)
    edge = jnp.where(lane < SUB, lane + rows - 3, lane - SUB)
    edge = jnp.where((lane % SUB < 3) & (lane < 2 * SUB), edge, -1)
    hit = (pos.astype(jnp.int32) == edge).astype(jnp.float32).astype(jnp.bfloat16)
    data = plain[:, : width * pieces]
    ends = as_bf16(over_rows(hit, data))
    ahead[...] = ends[:SUB]
    behind[...] = ends[SUB : 2 * SUB]
    sorted_rows[...] = as_bf16(over_rows(one_hot(pos), data))


def inner_kernel(rows_in, weight, x_project, dt_project, out, weight_here, x_here, dt_here, sems):
    parts = sems.shape[0] - 2
    width = weight.shape[1] // parts
    copies = []
    for k in range(parts):
        cols = pl.ds(k * width, width)
        copies.append((weight.at[:, cols], weight_here.at[:, cols]))
    copies += [(x_project, x_here), (dt_project, dt_here)]
    copies = [
        pltpu.make_async_copy(here, there, sems.at[k]) for k, (here, there) in enumerate(copies)
    ]
    for copy in copies:
        copy.start()
    for k in range(parts):
        cols = pl.ds(k * width, width)
        copies[k].wait()
        out[:, cols] = as_bf16(matmul(rows_in[...], weight_here[:, cols]))
    copies[parts].wait()
    copies[parts + 1].wait()


def sublane(shape):
    return lax.broadcasted_iota(jnp.int32, shape, 0)


def shift_sublanes(tile, count, reverse):
    return pltpu.roll(tile, SUB - count if reverse else count, 0)


def in_reach(count, reverse):
    row = sublane((SUB, LANES))
    return row < SUB - count if reverse else row >= count


def outside(total, reverse):
    for count in (1, 2, 4):
        moved = shift_sublanes(total, count, reverse)
        total = total + jnp.where(in_reach(count, reverse), moved, 0.0)
    return jnp.where(in_reach(1, reverse), shift_sublanes(total, 1, reverse), 0.0)


def tiles_of(array):
    return [array[SUB * t : SUB * t + SUB] for t in range(array.shape[0] // SUB)]


def in_order(count, reverse):
    return list(range(count))[::-1] if reverse else list(range(count))


def spread_columns(target, columns, first, count):
    for n in range(count):
        target[n] = jnp.broadcast_to(
            columns[:, first + n : first + n + 1], (columns.shape[0], LANES)
        )


def silu(v):
    half = 0.5 * v
    return half + half * jnp.tanh(half)


def halves(array):
    high = as_bf16(array)
    return high, as_bf16(array - high.astype(jnp.float32))


def sum_over_positions(columns, first, states):
    rows = columns.shape[0]
    size = (rows, rows * states)
    row = lax.broadcasted_iota(jnp.int32, size, 0)
    at = lax.broadcasted_iota(jnp.int32, size, 1)
    repeat = row == at // (PACK * states) * PACK + at % PACK
    repeat = repeat.astype(jnp.float32).astype(jnp.bfloat16)
    size = (states, rows * states)
    own = lax.broadcasted_iota(jnp.int32, size, 1) // PACK % states == sublane(size)
    parts = [
        as_bf16(jnp.where(own, matmul(part, repeat), 0.0))
        for part in halves(columns.T[first : first + states])
    ]
    return jnp.concatenate(parts, axis=0)


def in_fours(rows):
    count = rows.shape[0]
    size = (2 * count, count)
    out_row = sublane(size)
    wanted = out_row // 4 * 2 + out_row % 4
    pick = (wanted == lax.broadcasted_iota(jnp.int32, size, 1)) & (out_row % 4 < 2)
    return matmul(pick.astype(jnp.float32).astype(jnp.bfloat16), as_bf16(rows))


def paired(first, second):
    return as_bf16(jnp.concatenate([first, second], axis=0))


def sum_over_states(columns, first, states):
    rows = columns.shape[0]
    size = (columns.shape[1], PACK * states)
    col = lax.broadcasted_iota(jnp.int32, size, 0)
    at = lax.broadcasted_iota(jnp.int32, size, 1)
    repeat = (col == first + at // PACK).astype(jnp.float32).astype(jnp.bfloat16)
    size = (rows, PACK * states)
    row = lax.broadcasted_iota(jnp.int32, size, 0)
    at = lax.broadcasted_iota(jnp.int32, size, 1)
    own = row % PACK == at % PACK
    return [as_bf16(jnp.where(own, matmul(part, repeat), 0.0)) for part in halves(columns)]


def softplus(v):
    return jnp.maximum(v, 0.0) + jnp.log(1.0 + jnp.exp(-jnp.abs(v)))


def states_kernel(
    flags,
    inner_in,
    before,
    after,
    w_inner,
    conv_weight,
    conv_bias,
    x_project,
    dt_project,
    dt_bias,
    rates,
    u_result,
    proj_result,
    dt_result,
    payload_result,
    u_out,
    proj_out,
    dt_out,
    payload,
    left,
    edge_rows,
    extended,
    sems,
):
    copies = [
        pltpu.make_async_copy(here, there, sems.at[k])
        for k, (here, there) in enumerate(
            (
                (u_out, u_result),
                (proj_out, proj_result),
                (dt_out, dt_result),
                (payload.at[0], payload_result.at[0]),
                (payload.at[1], payload_result.at[1]),
            )
        )
    ]
    rows, channels = inner_in.shape
    taps = conv_weight.shape[1]
    reach = taps - 1
    width = extended.shape[1]
    states = rates.shape[1]
    rank = dt_project.shape[1]
    slots = rows // SUB
    tile = payload.shape[4]
    edge_rows[:SUB] = before[...]
    edge_rows[SUB:] = after[...]
    proj_out[...] = jnp.zeros_like(proj_out)

    def conv_block(step, carry):
        cols = pl.ds(pl.multiple_of(step * width, LANES), width)
        edges = as_bf16(matmul(edge_rows[...], w_inner[:, cols])).astype(jnp.float32)
        main = inner_in[:, cols].astype(jnp.float32)
        prior = edges[:SUB] * flags[0].astype(jnp.float32)
        later = edges[SUB:] * flags[1].astype(jnp.float32)
        row = sublane((SUB, width))
        extended[SUB * reach : SUB * reach + rows] = main
        for k in range(reach):
            own = main[rows - SUB * (reach - k) : rows - SUB * (reach - k - 1)]
            extended[SUB * k : SUB * k + SUB] = jnp.where(
                row == 0, prior[k : k + 1], pltpu.roll(own, 1, 0)
            )
            own = main[SUB * k : SUB * k + SUB]
            base = SUB * (reach + slots + k)
            extended[base : base + SUB] = jnp.where(
                row == SUB - 1, later[k : k + 1], pltpu.roll(own, SUB - 1, 0)
            )
        for d in range(2):
            mixed = conv_bias[d : d + 1, cols]
            for tap in range(taps):
                base = SUB * (2 * reach - tap if d else tap)
                gain = conv_weight[d, tap : tap + 1, cols]
                mixed = mixed + gain * extended[base : base + rows]
            u = as_bf16(silu(mixed))
            u_out[d, :, cols] = u
            proj_out[d] += matmul(u, x_project[d, cols, :])
        return carry

    lax.fori_loop(0, channels // width, conv_block, 0)
    copies[0].start()
    copies[1].start()
    for d in range(2):
        left[d] = sum_over_positions(proj_out[d], rank, states)

    def step_block(step, carry):
        cols = pl.ds(pl.multiple_of(step * width, LANES), width)
        for d in range(2):
            low = as_bf16(proj_out[d][:, :rank])
            raw = matmul(low, dt_project[d, :, cols])
            dt_out[d, :, cols] = softplus(raw + dt_bias[d : d + 1, cols])
        return carry

    lax.fori_loop(0, channels // width, step_block, 0)
    copies[2].start()
    def state_block(turn, carry):
        for pair in range(2):
            for d in range(2):
                first = turn * 4 + pair * 2
                sides = [
                    spans(pl.ds(pl.multiple_of((first + side) * LANES, LANES), LANES), d)
                    for side in range(2)
                ]
                out = None
                for k in range(slots // 2):
                    right = []
                    for n in range(states):
                        piece = []
                        for here, fed, rest, _ in sides:
                            rate = rates[d, n : n + 1, here]
                            piece.append(
                                paired(*(jnp.exp2(rest[t] * rate) * fed[t] for t in (2 * k, 2 * k + 1)))
                            )
                        right.append(jnp.concatenate(piece, axis=1))
                    size = PACK * states
                    part = matmul(
                        left[d, :, size * k : size * k + size], jnp.concatenate(right, axis=0)
                    )
                    out = part if out is None else out + part
                out = in_fours(out[:states] + out[states:])
                for side in range(2):
                    block = first + side
                    group = block // (tile // LANES)
                    within = pl.multiple_of((block - group * (tile // LANES)) * LANES, LANES)
                    for k in range(states // 2):
                        rows4 = out[4 * k : 4 * k + 4, side * LANES : side * LANES + LANES]
                        rows4 = jnp.where(sublane((4, LANES)) < 2, rows4, sides[side][3])
                        payload[d, k, group, :, pl.ds(within, LANES)] = as_bf16(rows4)
        return carry

    def spans(here, d):
        reverse = d == 1
        dt = dt_out[d, :, here]
        fed = tiles_of(dt * u_out[d, :, here].astype(jnp.float32))
        dt = tiles_of(dt)
        order = in_order(slots, not reverse)
        rest = {order[0]: None}
        total = dt[order[0]]
        for t in order[1:]:
            rest[t] = total
            total = total + dt[t]
        outer = outside(total, not reverse)
        whole = total + outer
        whole = whole[SUB - 1 : SUB] if reverse else whole[0:1]
        rest = {t: outer if part is None else part + outer for t, part in rest.items()}
        return here, fed, rest, whole

    lax.fori_loop(0, channels // (4 * LANES), state_block, 0)
    copies[3].start()
    copies[4].start()
    for copy in copies:
        copy.wait()


def local_kernel(dt_in, u_in, proj, rates, skip_gain, y_out, entry_out, b_wide, c_wide, *, reverse):
    d = int(reverse)
    states = rates.shape[1]
    rows, channels = y_out.shape
    slots = rows // SUB
    rank = proj.shape[2] - 2 * states

    @pl.when(pl.program_id(0) == 0)
    def _():
        spread_columns(b_wide, proj[0], rank, states)
        spread_columns(c_wide, proj[0], rank + states, states)

    def lane_block(block, carry):
        here = pl.ds(pl.multiple_of(block * LANES, LANES), LANES)
        dt = dt_in[0, :, here]
        u = u_in[0, :, here].astype(jnp.float32)
        fed = tiles_of(dt * u)
        dt = tiles_of(dt)
        gain = skip_gain[d : d + 1, here]
        sums = [gain * tile for tile in tiles_of(u)]
        total = dt[0]
        for t in range(1, slots):
            total = total + dt[t]
        for n in range(states):
            rate = rates[0, n : n + 1, here]
            state = None
            for t in in_order(slots, reverse):
                at = slice(SUB * t, SUB * t + SUB)
                new = fed[t] * b_wide[n, at]
                if state is not None:
                    new = jnp.exp2(dt[t] * rate) * state + new
                state = new
                sums[t] = sums[t] + c_wide[n, at] * state
            keep = jnp.exp2(total * rate)
            for count in (1, 2, 4):
                keep = jnp.where(in_reach(count, reverse), keep, 0.0)
                state = state + keep * shift_sublanes(state, count, reverse)
                if count < 4:
                    keep = keep * shift_sublanes(keep, count, reverse)
            near = in_reach(1, reverse)
            entry_out[n, :, here] = jnp.where(near, shift_sublanes(state, 1, reverse), 0.0)
        for t in range(slots):
            y_out[SUB * t : SUB * t + SUB, here] = sums[t]
        return carry

    lax.fori_loop(0, channels // LANES, lane_block, 0)


def relay_kernel(keep, payload, rates, entering):
    blocks = payload.shape[0]
    backward = keep[blocks]

    def block_step(i, state):
        at = jnp.where(backward == 1, blocks - 1 - i, i)
        state = state * keep[at].astype(jnp.float32)
        entering[at] = state.astype(jnp.bfloat16)
        row = payload[at].astype(jnp.float32)
        return jnp.exp2(rates[...] * row[2:3]) * state + row[0:2]

    lax.fori_loop(0, blocks, block_step, jnp.zeros(rates.shape, jnp.float32), unroll=16)


def outputs_kernel(
    entering,
    entry_fwd,
    entry_bwd,
    y_fwd,
    y_bwd,
    dt_in,
    proj,
    rates,
    places,
    out,
    left,
    placed,
):
    step = pl.program_id(0)
    states = rates.shape[1]
    rows, channels = y_fwd.shape
    slots = rows // SUB
    rank = proj.shape[2] - 2 * states
    tile = entering.shape[4]

    @pl.when(step == 0)
    def _():
        for d in range(2):
            parts = sum_over_states(proj[d], rank + states, states)
            for k in range(slots // 2):
                for i, part in enumerate(parts):
                    left[d, k, PACK * i : PACK * i + PACK] = part[PACK * k : PACK * k + PACK]

    def spans(at, d, entry):
        here = slice(at * LANES, at * LANES + LANES)
        block = step * (channels // LANES) + at
        group = block // (tile // LANES)
        within = pl.multiple_of((block - group * (tile // LANES)) * LANES, LANES)
        reverse = d == 1
        dt = tiles_of(dt_in[d, :, here])
        past = {}
        total = None
        for t in in_order(slots, reverse):
            total = dt[t] if total is None else total + dt[t]
            past[t] = total
        ahead = outside(total, reverse)
        entered = []
        for n in range(states):
            rate = rates[d, n : n + 1, here]
            pair = entering[d, n // 2, group, :, pl.ds(within, LANES)].astype(jnp.float32)
            entered.append(jnp.exp2(ahead * rate) * pair[n % 2 : n % 2 + 1] + entry[n, :, here])
        return here, past, entered

    pick = one_hot(places[...])
    for pair in range(channels // LANES // 2):
        cols = slice(pair * 2 * LANES, (pair + 1) * 2 * LANES)
        sums = y_fwd[:, cols] + y_bwd[:, cols]
        for d, entry in ((0, entry_fwd), (1, entry_bwd)):
            sides = [spans(2 * pair + side, d, entry) for side in range(2)]
            parts = []
            for k in range(slots // 2):
                right = []
                for n in range(states):
                    piece = []
                    for here, past, entered in sides:
                        rate = rates[d, n : n + 1, here]
                        piece.append(
                            paired(*(jnp.exp2(past[t] * rate) * entered[n] for t in (2 * k, 2 * k + 1)))
                        )
                    right.append(jnp.concatenate(piece, axis=1))
                part = matmul(left[d, k], jnp.concatenate(right, axis=0))
                parts.append(part[:PACK] + part[PACK:])
            sums = sums + jnp.concatenate(parts, axis=0)
        start = pl.multiple_of(step * channels + pair * 2 * LANES, 2 * LANES)
        placed[:, pl.ds(start, 2 * LANES)] = as_bf16(matmul(pick, as_bf16(sums)))

    @pl.when(step == pl.num_programs(0) - 1)
    def _():
        chunked([placed[:, tile * k : tile * k + tile] for k in range(SUB)], out)


def gate_kernel(returned, gate, out):
    rows = out.shape[0]
    group = rows // SUB
    width = returned.shape[1]
    gather = spread_index(rows, turned=True)
    for q in range(SUB):
        part = matmul(gather, returned[rows * q : rows * q + rows])
        here = slice(group * q, group * q + group)
        for k in range(SUB):
            cols = slice(width * k, width * k + width)
            out[here, cols] = as_bf16(part[group * k : group * k + group] * gate[here, cols])


def limits(mebibytes):
    return pltpu.CompilerParams(vmem_limit_bytes=mebibytes * 1024 * 1024)


def in_vmem(array):
    return pltpu.with_memory_space_constraint(array, pltpu.VMEM)


def in_hbm(array):
    return pltpu.with_memory_space_constraint(array, pltpu.HBM)


def on_chip(kernel, name, mebibytes, results, *operands, scalars=0, scratch=()):
    places = [pltpu.SMEM] * scalars + [pltpu.VMEM] * (len(operands) - scalars)
    one = pl.BlockSpec(memory_space=pltpu.VMEM)
    return pl.pallas_call(
        kernel,
        out_shape=results,
        in_specs=[pl.BlockSpec(memory_space=place) for place in places],
        out_specs=tuple(one for _ in results) if isinstance(results, tuple) else one,
        scratch_shapes=list(scratch),
        compiler_params=limits(mebibytes),
        name=name,
    )(
        *(
            in_vmem(operand) if place is pltpu.VMEM else operand
            for operand, place in zip(operands, places)
        )
    )


def local(
    tile_embed,
    destination,
    slide_lengths,
    w_inner,
    w_gate,
    conv_weight,
    conv_bias,
    x_project,
    dt_project,
    dt_bias,
    decay,
    skip_gain,
):
    f32, bf16 = jnp.float32, jnp.bfloat16
    shards = lax.axis_size(AXES)
    me = lax.axis_index(AXES)
    rows, model = tile_embed.shape
    width = w_inner.shape[1]
    states = decay.shape[1]
    rank = dt_project.shape[1]
    taps = conv_weight.shape[1]
    tile = 3 * LANES
    groups = width // tile
    owner_states = 2 * groups * states // shards
    state_groups = states // owner_states
    slots = rows // SUB

    blocks = jnp.arange(shards, dtype=jnp.int32)
    slide = jnp.arange(slide_lengths.shape[0], dtype=jnp.int32)
    ends = jnp.sum(jnp.where(slide[:, None] <= slide[None, :], slide_lengths[:, None], 0), axis=0)
    starts = ends - slide_lengths
    opens = jnp.any(blocks[:, None] * rows == starts[None, :], axis=1)
    closes = jnp.any((blocks[:, None] + 1) * rows == ends[None, :], axis=1)
    mine = blocks == me
    flags = jnp.stack([~jnp.any(opens & mine), ~jnp.any(closes & mine)]).astype(jnp.int32)
    owner_dir = me // (state_groups * groups)
    owner_group = (me // groups) % state_groups
    owner_tile = me % groups
    keep = jnp.where(owner_dir == 1, ~closes, ~opens).astype(jnp.int32)
    keep = jnp.concatenate([keep, jnp.full((SUB,), owner_dir, jnp.int32)])
    rates = decay * (-LOG2E)
    owner_rates = lax.dynamic_slice(
        rates, (owner_dir, owner_group * owner_states, owner_tile * tile), (1, owner_states, tile)
    )[0]

    piece = 2 * LANES
    sent = on_chip(
        pack_kernel, "pack", 3, pltpu.VMEM((SUB * rows, piece), bf16), tile_embed, destination[None, :]
    )
    arrived = lax.all_to_all(
        sent.reshape(rows, SUB, piece), AXES, split_axis=0, concat_axis=0, tiled=True
    ).reshape(SUB * rows, piece)
    gate = jax.nn.silu(jnp.dot(tile_embed, w_gate, preferred_element_type=f32))

    block_rows, ahead, behind, places = on_chip(
        sort_kernel,
        "sort_rows",
        4,
        (
            pltpu.VMEM((rows, model), bf16),
            pltpu.VMEM((SUB, model), bf16),
            pltpu.VMEM((SUB, model), bf16),
            pltpu.HBM((rows, LANES), f32),
        ),
        arrived,
        scratch=[pltpu.VMEM((rows, model + piece), bf16)],
    )
    before = lax.ppermute(ahead, AXES, [(i, i + 1) for i in range(shards - 1)])
    after = lax.ppermute(behind, AXES, [(i + 1, i) for i in range(shards - 1)])
    hbm_spec = pl.BlockSpec(memory_space=pltpu.HBM)
    vmem_spec = pl.BlockSpec(memory_space=pltpu.VMEM)
    weights = (w_inner, x_project, dt_project)
    inner, w_inner, x_project, dt_project = pl.pallas_call(
        inner_kernel,
        out_shape=(
            pltpu.VMEM((rows, width), bf16),
            *(pltpu.VMEM(w.shape, w.dtype) for w in weights),
        ),
        in_specs=[vmem_spec] + [hbm_spec] * 3,
        out_specs=(vmem_spec,) * 4,
        scratch_shapes=[pltpu.SemaphoreType.DMA((6,))],
        compiler_params=limits(2),
        name="inner",
    )(in_vmem(block_rows), *(in_hbm(w) for w in weights))

    operands = (
        inner, before, after, w_inner, conv_weight, conv_bias, x_project, dt_project, dt_bias, rates,
    )
    on_chip_results = [
        pltpu.VMEM((2, rows, width), bf16),
        pltpu.VMEM((2, rows, LANES), f32),
        pltpu.VMEM((2, rows, width), f32),
        pltpu.VMEM((2, state_groups, groups, 4, tile), bf16),
        pltpu.VMEM((2, 2 * states, rows * states), bf16),
    ]
    u, proj, dt, payload = pl.pallas_call(
        states_kernel,
        out_shape=(
            pltpu.HBM((2, rows, width), bf16),
            pltpu.HBM((2, rows, LANES), f32),
            pltpu.HBM((2, rows, width), f32),
            pltpu.HBM((2, state_groups, groups, 4, tile), bf16),
        ),
        in_specs=[pl.BlockSpec(memory_space=pltpu.SMEM)] + [vmem_spec] * len(operands),
        out_specs=(hbm_spec,) * 4,
        scratch_shapes=on_chip_results
        + [
            pltpu.VMEM((2 * SUB, model), bf16),
            pltpu.VMEM((rows + 2 * SUB * (taps - 1), 2 * tile), f32),
            pltpu.SemaphoreType.DMA((5,)),
        ],
        compiler_params=limits(14),
        name="block_states",
    )(flags, *(in_vmem(operand) for operand in operands))

    def local_outputs(d):
        return pl.pallas_call(
            functools.partial(local_kernel, reverse=d == 1),
            out_shape=(
                pltpu.HBM((rows, width), f32),
                pltpu.HBM((states, SUB, width), f32),
            ),
            grid=(groups,),
            in_specs=[
                pl.BlockSpec((1, rows, tile), lambda i: (d, 0, i)),
                pl.BlockSpec((1, rows, tile), lambda i: (d, 0, i)),
                pl.BlockSpec((1, rows, LANES), lambda i: (d, 0, 0)),
                pl.BlockSpec((1, states, tile), lambda i: (d, 0, i)),
                pl.BlockSpec((2, tile), lambda i: (0, i)),
            ],
            out_specs=[
                pl.BlockSpec((rows, tile), lambda i: (0, i)),
                pl.BlockSpec((states, SUB, tile), lambda i: (0, 0, i)),
            ],
            scratch_shapes=[pltpu.VMEM((states, rows, LANES), f32)] * 2,
            compiler_params=limits(6),
            name="local_bwd_outputs" if d else "local_fwd_outputs",
        )(in_hbm(dt), in_hbm(u), in_hbm(proj), rates, skip_gain)

    local_fwd = local_outputs(0)
    local_bwd = local_outputs(1)

    shared = lax.all_to_all(
        payload.reshape(shards, 4, tile), AXES, split_axis=0, concat_axis=0, tiled=True
    )
    shared, *local_fwd = lax.optimization_barrier((shared, *local_fwd))
    entering = on_chip(
        relay_kernel,
        "relay",
        2,
        pltpu.VMEM((shards, owner_states, tile), bf16),
        keep, shared, owner_rates,
        scalars=1,
    )
    entering = lax.all_to_all(entering, AXES, split_axis=0, concat_axis=0, tiled=True)
    entering, *local_bwd = lax.optimization_barrier((entering, *local_bwd))
    entering = entering.reshape(2, state_groups, groups, owner_states, tile)
    y_fwd, entry_fwd = local_fwd
    y_bwd, entry_bwd = local_bwd

    part = 4 * LANES
    totals = pl.pallas_call(
        outputs_kernel,
        out_shape=pltpu.HBM((SUB * rows, tile), bf16),
        grid=(width // part,),
        in_specs=[
            vmem_spec,
            pl.BlockSpec((states, SUB, part), lambda i: (0, 0, i)),
            pl.BlockSpec((states, SUB, part), lambda i: (0, 0, i)),
            pl.BlockSpec((rows, part), lambda i: (0, i)),
            pl.BlockSpec((rows, part), lambda i: (0, i)),
            pl.BlockSpec((2, rows, part), lambda i: (0, 0, i)),
            pl.BlockSpec((2, rows, LANES), lambda i: (0, 0, 0)),
            pl.BlockSpec((2, states, part), lambda i: (0, 0, i)),
            pl.BlockSpec((rows, LANES), lambda i: (0, 0)),
        ],
        out_specs=pl.BlockSpec((SUB * rows, tile), lambda i: (0, 0)),
        scratch_shapes=[
            pltpu.VMEM((2, slots // 2, 2 * PACK, PACK * states), bf16),
            pltpu.VMEM((rows, width), bf16),
        ],
        compiler_params=limits(12),
        name="block_outputs",
    )(
        in_vmem(entering),
        *(in_hbm(array) for array in (entry_fwd, entry_bwd, y_fwd, y_bwd, dt, proj)),
        rates,
        in_hbm(places),
    )

    returned = lax.all_to_all(
        totals.reshape(rows, SUB, tile), AXES, split_axis=0, concat_axis=0, tiled=True
    ).reshape(SUB * rows, tile)
    return pl.pallas_call(
        gate_kernel,
        out_shape=jax.ShapeDtypeStruct((rows, width), bf16),
        compiler_params=limits(5),
        name="gated",
    )(in_vmem(returned), gate)


def solution(mesh):
    placed = (P(AXES, None), P(AXES)) + (P(),) * 10
    return jax.shard_map(
        local, mesh=mesh, in_specs=placed, out_specs=P(AXES, None), check_vma=False
    )
```

```python
import functools

import jax
import jax.numpy as jnp
from jax import lax
from jax.experimental import pallas as pl
from jax.experimental.pallas import tpu as pltpu
from jax.sharding import PartitionSpec as P

AXES = ("seq", "slide")
SUB = 8
LANES = 128
PACK = 16
LOG2E = 1.4426950408889634


def spread_index(rows, turned=False):
    shape = (rows, rows)
    row = lax.broadcasted_iota(jnp.int32, shape, 1 if turned else 0)
    col = lax.broadcasted_iota(jnp.int32, shape, 0 if turned else 1)
    group = rows // SUB
    hit = (row // SUB == col % group) & (row % SUB == col // group)
    return hit.astype(jnp.float32).astype(jnp.bfloat16)


def as_bf16(product):
    return product.astype(jnp.bfloat16)


def matmul(left, right):
    return jnp.dot(left, right, preferred_element_type=jnp.float32)


def over_rows(left, right):
    return lax.dot_general(
        left, right, (((0,), (0,)), ((), ())), preferred_element_type=jnp.float32
    )


def chunked(pieces, out):
    rows = pieces[0].shape[0]
    group = rows // SUB
    spread = spread_index(rows)
    blank = [jnp.zeros_like(pieces[0])] * (SUB - len(pieces))
    for q in range(SUB):
        part = [piece[group * q : group * q + group] for piece in list(pieces) + blank]
        out[rows * q : rows * q + rows] = as_bf16(matmul(spread, jnp.concatenate(part, axis=0)))


def pack_kernel(embed, destination, out):
    rows = embed.shape[0]
    width = out.shape[1]
    pieces = [embed[:, at : at + width] for at in range(0, embed.shape[1], width)]
    row = lax.broadcasted_iota(jnp.int32, (rows, rows), 0)
    col = lax.broadcasted_iota(jnp.int32, (rows, rows), 1)
    offset = jnp.where(row == col, destination[...] - rows * col, 0)
    offset = as_bf16(offset.astype(jnp.float32))
    pieces.append(as_bf16(matmul(offset, jnp.ones((rows, width), jnp.bfloat16))))
    chunked(pieces, out)


def row_positions(shape, per_sub):
    lane = lax.broadcasted_iota(jnp.int32, shape, 1)
    return (lane % SUB) * per_sub + lane // SUB


def one_hot(pos):
    place = row_positions(pos.shape, pos.shape[1] // SUB)
    hit = pos.astype(jnp.int32) == place
    return hit.astype(jnp.float32).astype(jnp.bfloat16)


def sort_kernel(arrived, sorted_rows, ahead, behind, places, plain):
    rows = sorted_rows.shape[0]
    group = rows // SUB
    width = arrived.shape[1]
    pieces = sorted_rows.shape[1] // width
    gather = spread_index(rows, turned=True)
    for q in range(SUB):
        part = as_bf16(matmul(gather, arrived[rows * q : rows * q + rows]))
        for k in range(pieces + 1):
            plain[group * q : group * q + group, width * k : width * k + width] = part[
                group * k : group * k + group
            ]
    pos = plain[:, width * pieces : width * pieces + LANES].astype(jnp.float32)
    places[...] = pos
    lane = lax.broadcasted_iota(jnp.int32, pos.shape, 1)
    edge = jnp.where(lane < SUB, lane + rows - 3, lane - SUB)
    edge = jnp.where((lane % SUB < 3) & (lane < 2 * SUB), edge, -1)
    hit = (pos.astype(jnp.int32) == edge).astype(jnp.float32).astype(jnp.bfloat16)
    data = plain[:, : width * pieces]
    ends = as_bf16(over_rows(hit, data))
    ahead[...] = ends[:SUB]
    behind[...] = ends[SUB : 2 * SUB]
    sorted_rows[...] = as_bf16(over_rows(one_hot(pos), data))


def inner_kernel(
    rows_in,
    conv_weight,
    conv_bias,
    weight,
    x_project,
    dt_project,
    u_out,
    proj_out,
    edge_sums,
    weight_here,
    x_here,
    dt_here,
    extended,
    sems,
):
    parts = sems.shape[0] - 2
    width = weight.shape[1] // parts
    rows = rows_in.shape[0]
    taps = conv_weight.shape[1]
    reach = taps - 1
    slots = rows // SUB
    moves = []
    for k in range(parts):
        cols = pl.ds(k * width, width)
        moves.append((weight.at[:, cols], weight_here.at[:, cols]))
        if k == 0:
            moves.append((x_project, x_here))
    moves.append((dt_project, dt_here))
    copies = [
        pltpu.make_async_copy(here, there, sems.at[k]) for k, (here, there) in enumerate(moves)
    ]
    for copy in copies:
        copy.start()
    proj_out[...] = jnp.zeros_like(proj_out)
    row = sublane((SUB, width))
    for k in range(parts):
        cols = slice(k * width, k * width + width)
        if k == 0:
            copies[0].wait()
            copies[1].wait()
        else:
            copies[k + 1].wait()
        main = as_bf16(matmul(rows_in[...], weight_here[:, cols])).astype(jnp.float32)
        extended[SUB * reach : SUB * reach + rows] = main
        for i in range(reach):
            own = main[rows - SUB * (reach - i) : rows - SUB * (reach - i - 1)]
            extended[SUB * i : SUB * i + SUB] = jnp.where(row == 0, 0.0, pltpu.roll(own, 1, 0))
            own = main[SUB * i : SUB * i + SUB]
            base = SUB * (reach + slots + i)
            extended[base : base + SUB] = jnp.where(
                row == SUB - 1, 0.0, pltpu.roll(own, SUB - 1, 0)
            )
        for d in range(2):
            mixed = conv_bias[d : d + 1, cols]
            for tap in range(taps):
                base = SUB * (2 * reach - tap if d else tap)
                mixed = mixed + conv_weight[d, tap : tap + 1, cols] * extended[base : base + rows]
            edge = SUB * reach
            edge_sums[d, :, cols] = mixed[rows - edge :] if d else mixed[:edge]
            u = as_bf16(silu(mixed))
            u_out[d, :, cols] = u
            proj_out[d] += matmul(u, x_here[d, cols, :])
    copies[parts + 1].wait()


def sublane(shape):
    return lax.broadcasted_iota(jnp.int32, shape, 0)


def shift_sublanes(tile, count, reverse):
    return pltpu.roll(tile, SUB - count if reverse else count, 0)


def in_reach(count, reverse):
    row = sublane((SUB, LANES))
    return row < SUB - count if reverse else row >= count


def outside(total, reverse):
    for count in (1, 2, 4):
        moved = shift_sublanes(total, count, reverse)
        total = total + jnp.where(in_reach(count, reverse), moved, 0.0)
    return jnp.where(in_reach(1, reverse), shift_sublanes(total, 1, reverse), 0.0)


def tiles_of(array):
    return [array[SUB * t : SUB * t + SUB] for t in range(array.shape[0] // SUB)]


def in_order(count, reverse):
    return list(range(count))[::-1] if reverse else list(range(count))


def spread_columns(target, columns, first, count):
    for n in range(count):
        target[n] = jnp.broadcast_to(
            columns[:, first + n : first + n + 1], (columns.shape[0], LANES)
        )


def silu(v):
    half = 0.5 * v
    return half + half * jnp.tanh(half)


def halves(array):
    high = as_bf16(array)
    return high, as_bf16(array - high.astype(jnp.float32))


def paired(first, second):
    return as_bf16(jnp.concatenate([first, second], axis=0))


def sum_over_states(columns, first, states):
    rows = columns.shape[0]
    size = (columns.shape[1], PACK * states)
    col = lax.broadcasted_iota(jnp.int32, size, 0)
    at = lax.broadcasted_iota(jnp.int32, size, 1)
    repeat = (col == first + at // PACK).astype(jnp.float32).astype(jnp.bfloat16)
    size = (rows, PACK * states)
    row = lax.broadcasted_iota(jnp.int32, size, 0)
    at = lax.broadcasted_iota(jnp.int32, size, 1)
    own = row % PACK == at % PACK
    return [as_bf16(jnp.where(own, matmul(part, repeat), 0.0)) for part in halves(columns)]


def softplus(v):
    return jnp.maximum(v, 0.0) + jnp.log(1.0 + jnp.exp(-jnp.abs(v)))


def states_kernel(
    flags,
    proj_in,
    edge_sums,
    before,
    after,
    w_inner,
    conv_weight,
    x_project,
    dt_project,
    dt_bias,
    rates,
    u_in,
    u_result,
    proj_result,
    dt_result,
    payload_result,
    entry_result,
    u_out,
    proj_out,
    dt_out,
    payload,
    entry,
    b_wide,
    edge_rows,
    sems,
):
    copies = [
        pltpu.make_async_copy(here, there, sems.at[k])
        for k, (here, there) in enumerate(
            (
                (u_out, u_result),
                (proj_out, proj_result),
                (dt_out, dt_result),
                (payload.at[0], payload_result.at[0]),
                (payload.at[1], payload_result.at[1]),
            )
        )
    ]
    _, rows, channels = u_out.shape
    taps = conv_weight.shape[1]
    reach = taps - 1
    width = channels // 4
    states = rates.shape[1]
    rank = dt_project.shape[1]
    slots = rows // SUB
    tile = payload.shape[4]
    edge = SUB * reach
    edge_rows[:SUB] = before[...]
    edge_rows[SUB:] = after[...]
    row = sublane((SUB, width))
    projected = [jnp.zeros((edge, LANES), jnp.float32)] * 2
    for step in range(channels // width):
        cols = slice(step * width, step * width + width)
        edges = as_bf16(matmul(edge_rows[...], w_inner[:, cols])).astype(jnp.float32)
        prior = edges[:SUB] * flags[0].astype(jnp.float32)
        later = edges[SUB:] * flags[1].astype(jnp.float32)
        for d in range(2):
            tiles = []
            for m in range(reach):
                if d:
                    terms = [(tap, later[m - tap : m - tap + 1]) for tap in range(m + 1)]
                else:
                    terms = [(tap, prior[m + tap : m + tap + 1]) for tap in range(reach - m)]
                extra = sum(conv_weight[d, tap : tap + 1, cols] * term for tap, term in terms)
                mixed = edge_sums[d, SUB * m : SUB * m + SUB, cols]
                tiles.append(mixed + jnp.where(row == (SUB - 1 if d else 0), extra, 0.0))
            u = as_bf16(silu(jnp.concatenate(tiles, axis=0)))
            first = rows - edge if d else 0
            u_out[d, first : first + edge, cols] = u
            projected[d] = projected[d] + matmul(u, x_project[d, cols, :])
    copies[0].start()
    for d in range(2):
        proj_out[d] = proj_in[d]
        first = rows - edge if d else 0
        proj_out[d, first : first + edge] = projected[d]
    copies[1].start()
    for d in range(2):
        spread_columns(b_wide.at[d], proj_out[d], rank, states)

    def step_block(step, carry):
        cols = pl.ds(pl.multiple_of(step * width, LANES), width)
        for d in range(2):
            low = as_bf16(proj_out[d][:, :rank])
            raw = matmul(low, dt_project[d, :, cols])
            dt_out[d, :, cols] = softplus(raw + dt_bias[d : d + 1, cols])
        return carry

    lax.fori_loop(0, channels // width, step_block, 0)
    copies[2].start()
    row = sublane((SUB, LANES))

    def state_block(block, carry, d):
        here = pl.ds(pl.multiple_of(block * LANES, LANES), LANES)
        group = block // (tile // LANES)
        within = pl.multiple_of((block - group * (tile // LANES)) * LANES, LANES)
        reverse = d == 1
        dt = dt_out[d, :, here]
        fed = tiles_of(dt * u_out[d, :, here].astype(jnp.float32))
        dt = tiles_of(dt)
        total = dt[0]
        for t in range(1, slots):
            total = total + dt[t]
        near = in_reach(1, reverse)
        finals = []
        for n in range(states):
            rate = rates[d, n : n + 1, here]
            state = None
            for t in in_order(slots, reverse):
                new = fed[t] * b_wide[d, n, SUB * t : SUB * t + SUB]
                if state is not None:
                    new = jnp.exp2(dt[t] * rate) * state + new
                state = new
            keep = jnp.exp2(total * rate)
            for count in (1, 2, 4):
                keep = jnp.where(in_reach(count, reverse), keep, 0.0)
                state = state + keep * shift_sublanes(state, count, reverse)
                if count < 4:
                    keep = keep * shift_sublanes(keep, count, reverse)
            entry[d, n, :, here] = jnp.where(near, shift_sublanes(state, 1, reverse), 0.0)
            finals.append(state[0:1] if reverse else state[SUB - 1 : SUB])
        whole = jnp.sum(total, axis=0, keepdims=True)
        for n in range(0, states, 2):
            out = jnp.where(row == 0, finals[n], finals[n + 1])
            out = jnp.where(row >= 2, whole, out)
            payload[d, n // 2, group, :, pl.ds(within, LANES)] = as_bf16(out[:4])
        return carry

    thirds = channels // LANES // 3
    for d in range(2):
        for part in range(3):
            body = functools.partial(state_block, d=d)
            lax.fori_loop(part * thirds, part * thirds + thirds, body, 0)
            cols = pl.ds(part * thirds * LANES, thirds * LANES)
            copies.append(
                pltpu.make_async_copy(
                    entry.at[d, :, :, cols],
                    entry_result.at[d, :, :, cols],
                    sems.at[5 + 3 * d + part],
                )
            )
            copies[-1].start()
        copies[3 + d].start()
    for copy in copies:
        copy.wait()


def relay_kernel(keep, payload, rates, entering):
    blocks = payload.shape[0]
    backward = keep[blocks]

    def block_step(i, state):
        at = jnp.where(backward == 1, blocks - 1 - i, i)
        state = state * keep[at].astype(jnp.float32)
        entering[at] = state.astype(jnp.bfloat16)
        row = payload[at].astype(jnp.float32)
        return jnp.exp2(rates[...] * row[2:3]) * state + row[0:2]

    lax.fori_loop(0, blocks, block_step, jnp.zeros(rates.shape, jnp.float32), unroll=16)


def outputs_kernel(
    entering,
    entry,
    dt_in,
    u_in,
    proj,
    rates,
    skip_gain,
    places,
    out,
    left,
    b_wide,
    placed,
):
    step = pl.program_id(0)
    states = rates.shape[1]
    _, rows, channels = dt_in.shape
    slots = rows // SUB
    rank = proj.shape[2] - 2 * states
    tile = entering.shape[4]

    @pl.when(step == 0)
    def _():
        for d in range(2):
            spread_columns(b_wide.at[d], proj[d], rank, states)
            parts = sum_over_states(proj[d], rank + states, states)
            for k in range(slots // 2):
                for i, part in enumerate(parts):
                    left[d, k, PACK * i : PACK * i + PACK] = part[PACK * k : PACK * k + PACK]

    def swept(at, d):
        here = slice(at * LANES, at * LANES + LANES)
        block = step * (channels // LANES) + at
        group = block // (tile // LANES)
        within = pl.multiple_of((block - group * (tile // LANES)) * LANES, LANES)
        reverse = d == 1
        dt = dt_in[d, :, here]
        u = u_in[d, :, here].astype(jnp.float32)
        fed = tiles_of(dt * u)
        dt = tiles_of(dt)
        total = dt[0]
        for t in range(1, slots):
            total = total + dt[t]
        ahead = outside(total, reverse)
        state = []
        for n in range(states):
            pair = entering[d, n // 2, group, :, pl.ds(within, LANES)].astype(jnp.float32)
            carried = jnp.exp2(ahead * rates[d, n : n + 1, here]) * pair[n % 2 : n % 2 + 1]
            state.append(carried + entry[d, n, :, here])
        sums = [None] * (slots // 2)
        for k in in_order(slots // 2, reverse):
            right = []
            for n in range(states):
                rate = rates[d, n : n + 1, here]
                both = []
                for t in in_order(2, reverse):
                    t = 2 * k + t
                    new = fed[t] * b_wide[d, n, SUB * t : SUB * t + SUB]
                    state[n] = jnp.exp2(dt[t] * rate) * state[n] + new
                    both.append(state[n])
                right.append(paired(*(both[::-1] if reverse else both)))
            part = matmul(left[d, k], jnp.concatenate(right, axis=0))
            sums[k] = part[:PACK] + part[PACK:]
        return jnp.concatenate(sums, axis=0) + skip_gain[d : d + 1, here] * u

    pick = one_hot(places[...])
    for at in range(channels // LANES):
        total = swept(at, 0) + swept(at, 1)
        start = pl.multiple_of(step * channels + at * LANES, LANES)
        placed[:, pl.ds(start, LANES)] = as_bf16(matmul(pick, as_bf16(total)))

    @pl.when(step == pl.num_programs(0) - 1)
    def _():
        chunked([placed[:, tile * k : tile * k + tile] for k in range(SUB)], out)


def gate_kernel(returned, gate, out):
    rows = out.shape[0]
    group = rows // SUB
    width = returned.shape[1]
    gather = spread_index(rows, turned=True)
    for q in range(SUB):
        part = matmul(gather, returned[rows * q : rows * q + rows])
        here = slice(group * q, group * q + group)
        for k in range(SUB):
            cols = slice(width * k, width * k + width)
            out[here, cols] = as_bf16(part[group * k : group * k + group] * gate[here, cols])


def limits(mebibytes):
    return pltpu.CompilerParams(vmem_limit_bytes=mebibytes * 1024 * 1024)


def in_vmem(array):
    return pltpu.with_memory_space_constraint(array, pltpu.VMEM)


def in_hbm(array):
    return pltpu.with_memory_space_constraint(array, pltpu.HBM)


def on_chip(kernel, name, mebibytes, results, *operands, scalars=0, scratch=()):
    places = [pltpu.SMEM] * scalars + [pltpu.VMEM] * (len(operands) - scalars)
    one = pl.BlockSpec(memory_space=pltpu.VMEM)
    return pl.pallas_call(
        kernel,
        out_shape=results,
        in_specs=[pl.BlockSpec(memory_space=place) for place in places],
        out_specs=tuple(one for _ in results) if isinstance(results, tuple) else one,
        scratch_shapes=list(scratch),
        compiler_params=limits(mebibytes),
        name=name,
    )(
        *(
            in_vmem(operand) if place is pltpu.VMEM else operand
            for operand, place in zip(operands, places)
        )
    )


def local(
    tile_embed,
    destination,
    slide_lengths,
    w_inner,
    w_gate,
    conv_weight,
    conv_bias,
    x_project,
    dt_project,
    dt_bias,
    decay,
    skip_gain,
):
    f32, bf16 = jnp.float32, jnp.bfloat16
    shards = lax.axis_size(AXES)
    me = lax.axis_index(AXES)
    rows, model = tile_embed.shape
    width = w_inner.shape[1]
    states = decay.shape[1]
    rank = dt_project.shape[1]
    taps = conv_weight.shape[1]
    tile = 3 * LANES
    groups = width // tile
    owner_states = 2 * groups * states // shards
    state_groups = states // owner_states
    slots = rows // SUB

    blocks = jnp.arange(shards, dtype=jnp.int32)
    slide = jnp.arange(slide_lengths.shape[0], dtype=jnp.int32)
    ends = jnp.sum(jnp.where(slide[:, None] <= slide[None, :], slide_lengths[:, None], 0), axis=0)
    starts = ends - slide_lengths
    opens = jnp.any(blocks[:, None] * rows == starts[None, :], axis=1)
    closes = jnp.any((blocks[:, None] + 1) * rows == ends[None, :], axis=1)
    mine = blocks == me
    flags = jnp.stack([~jnp.any(opens & mine), ~jnp.any(closes & mine)]).astype(jnp.int32)
    owner_dir = me // (state_groups * groups)
    owner_group = (me // groups) % state_groups
    owner_tile = me % groups
    keep = jnp.where(owner_dir == 1, ~closes, ~opens).astype(jnp.int32)
    keep = jnp.concatenate([keep, jnp.full((SUB,), owner_dir, jnp.int32)])
    rates = decay * (-LOG2E)
    owner_rates = lax.dynamic_slice(
        rates, (owner_dir, owner_group * owner_states, owner_tile * tile), (1, owner_states, tile)
    )[0]

    piece = 2 * LANES
    sent = pl.pallas_call(
        pack_kernel,
        out_shape=pltpu.VMEM((SUB * rows, piece), bf16),
        compiler_params=limits(3),
        name="pack",
    )(in_hbm(tile_embed), in_hbm(destination[None, :]))
    arrived = lax.all_to_all(
        sent.reshape(rows, SUB, piece), AXES, split_axis=0, concat_axis=0, tiled=True
    ).reshape(SUB * rows, piece)
    gate = jax.nn.silu(jnp.dot(tile_embed, w_gate, preferred_element_type=f32))

    block_rows, ahead, behind, places = on_chip(
        sort_kernel,
        "sort_rows",
        4,
        (
            pltpu.VMEM((rows, model), bf16),
            pltpu.VMEM((SUB, model), bf16),
            pltpu.VMEM((SUB, model), bf16),
            pltpu.HBM((rows, LANES), f32),
        ),
        arrived,
        scratch=[pltpu.VMEM((rows, model + piece), bf16)],
    )
    before = lax.ppermute(ahead, AXES, [(i, i + 1) for i in range(shards - 1)])
    after = lax.ppermute(behind, AXES, [(i + 1, i) for i in range(shards - 1)])
    hbm_spec = pl.BlockSpec(memory_space=pltpu.HBM)
    vmem_spec = pl.BlockSpec(memory_space=pltpu.VMEM)
    weights = (w_inner, x_project, dt_project)
    edge = SUB * (taps - 1)
    results = (
        pltpu.VMEM((2, rows, width), bf16),
        pltpu.VMEM((2, rows, LANES), f32),
        pltpu.VMEM((2, edge, width), f32),
        *(pltpu.VMEM(w.shape, w.dtype) for w in weights),
    )
    u, proj, edge_sums, w_inner, x_project, dt_project = pl.pallas_call(
        inner_kernel,
        out_shape=results,
        in_specs=[vmem_spec] * 3 + [hbm_spec] * 3,
        out_specs=(vmem_spec,) * len(results),
        scratch_shapes=[
            pltpu.VMEM((rows + 2 * edge, width // 4), f32),
            pltpu.SemaphoreType.DMA((6,)),
        ],
        compiler_params=limits(4),
        name="inner",
    )(
        *(in_vmem(operand) for operand in (block_rows, conv_weight, conv_bias)),
        *(in_hbm(w) for w in weights),
    )

    operands = (
        proj, edge_sums, before, after, w_inner, conv_weight, x_project, dt_project, dt_bias, rates, u,
    )
    on_chip_results = [
        pltpu.VMEM((2, rows, LANES), f32),
        pltpu.VMEM((2, rows, width), f32),
        pltpu.VMEM((2, state_groups, groups, 4, tile), bf16),
        pltpu.VMEM((2, states, SUB, width), f32),
        pltpu.VMEM((2, states, rows, LANES), f32),
    ]
    u, proj, dt, payload, entry, _ = pl.pallas_call(
        states_kernel,
        out_shape=(
            pltpu.HBM((2, rows, width), bf16),
            pltpu.HBM((2, rows, LANES), f32),
            pltpu.HBM((2, rows, width), f32),
            pltpu.HBM((2, state_groups, groups, 4, tile), bf16),
            pltpu.HBM((2, states, SUB, width), f32),
            pltpu.VMEM((2, rows, width), bf16),
        ),
        in_specs=[pl.BlockSpec(memory_space=pltpu.SMEM)] + [vmem_spec] * len(operands),
        out_specs=(hbm_spec,) * 5 + (vmem_spec,),
        input_output_aliases={len(operands): 5},
        scratch_shapes=on_chip_results
        + [
            pltpu.VMEM((2 * SUB, model), bf16),
            pltpu.SemaphoreType.DMA((11,)),
        ],
        compiler_params=limits(14),
        name="block_states",
    )(flags, *(in_vmem(operand) for operand in operands))

    shared = lax.all_to_all(
        payload.reshape(shards, 4, tile), AXES, split_axis=0, concat_axis=0, tiled=True
    )
    entering = on_chip(
        relay_kernel,
        "relay",
        2,
        pltpu.VMEM((shards, owner_states, tile), bf16),
        keep, shared, owner_rates,
        scalars=1,
    )
    entering = lax.all_to_all(entering, AXES, split_axis=0, concat_axis=0, tiled=True)
    entering = entering.reshape(2, state_groups, groups, owner_states, tile)

    part = 4 * LANES
    totals = pl.pallas_call(
        outputs_kernel,
        out_shape=pltpu.HBM((SUB * rows, tile), bf16),
        grid=(width // part,),
        in_specs=[
            vmem_spec,
            pl.BlockSpec((2, states, SUB, part), lambda i: (0, 0, 0, i)),
            pl.BlockSpec((2, rows, part), lambda i: (0, 0, i)),
            pl.BlockSpec((2, rows, part), lambda i: (0, 0, i)),
            pl.BlockSpec((2, rows, LANES), lambda i: (0, 0, 0)),
            pl.BlockSpec((2, states, part), lambda i: (0, 0, i)),
            pl.BlockSpec((2, part), lambda i: (0, i)),
            pl.BlockSpec((rows, LANES), lambda i: (0, 0)),
        ],
        out_specs=pl.BlockSpec((SUB * rows, tile), lambda i: (0, 0)),
        scratch_shapes=[
            pltpu.VMEM((2, slots // 2, 2 * PACK, PACK * states), bf16),
            pltpu.VMEM((2, states, rows, LANES), f32),
            pltpu.VMEM((rows, width), bf16),
        ],
        compiler_params=limits(12),
        name="block_outputs",
    )(
        in_vmem(entering),
        *(in_hbm(array) for array in (entry, dt, u, proj)),
        rates,
        skip_gain,
        in_hbm(places),
    )

    returned = lax.all_to_all(
        totals.reshape(rows, SUB, tile), AXES, split_axis=0, concat_axis=0, tiled=True
    ).reshape(SUB * rows, tile)
    return pl.pallas_call(
        gate_kernel,
        out_shape=jax.ShapeDtypeStruct((rows, width), bf16),
        compiler_params=limits(5),
        name="gated",
    )(in_vmem(returned), gate)


def solution(mesh):
    placed = (P(AXES, None), P(AXES)) + (P(),) * 10
    return jax.shard_map(
        local, mesh=mesh, in_specs=placed, out_specs=P(AXES, None), check_vma=False
    )
```

```python
import functools

import jax
import jax.numpy as jnp
from jax import lax
from jax.experimental import pallas as pl
from jax.experimental.pallas import tpu as pltpu
from jax.sharding import PartitionSpec as P

AXES = ("seq", "slide")
SUB = 8
LANES = 128
PACK = 16
LOG2E = 1.4426950408889634


def spread_index(rows, turned=False):
    shape = (rows, rows)
    row = lax.broadcasted_iota(jnp.int32, shape, 1 if turned else 0)
    col = lax.broadcasted_iota(jnp.int32, shape, 0 if turned else 1)
    group = rows // SUB
    hit = (row // SUB == col % group) & (row % SUB == col // group)
    return hit.astype(jnp.float32).astype(jnp.bfloat16)


def as_bf16(product):
    return product.astype(jnp.bfloat16)


def matmul(left, right):
    return jnp.dot(left, right, preferred_element_type=jnp.float32)


def over_rows(left, right):
    return lax.dot_general(
        left, right, (((0,), (0,)), ((), ())), preferred_element_type=jnp.float32
    )


def chunked(pieces, out):
    rows = pieces[0].shape[0]
    group = rows // SUB
    spread = spread_index(rows)
    blank = [jnp.zeros_like(pieces[0])] * (SUB - len(pieces))
    for q in range(SUB):
        part = [piece[group * q : group * q + group] for piece in list(pieces) + blank]
        out[rows * q : rows * q + rows] = as_bf16(matmul(spread, jnp.concatenate(part, axis=0)))


def pack_kernel(embed, destination, out):
    rows = embed.shape[0]
    width = out.shape[1]
    pieces = [embed[:, at : at + width] for at in range(0, embed.shape[1], width)]
    row = lax.broadcasted_iota(jnp.int32, (rows, rows), 0)
    col = lax.broadcasted_iota(jnp.int32, (rows, rows), 1)
    offset = jnp.where(row == col, destination[...] - rows * col, 0)
    offset = as_bf16(offset.astype(jnp.float32))
    pieces.append(as_bf16(matmul(offset, jnp.ones((rows, width), jnp.bfloat16))))
    chunked(pieces, out)


def row_positions(shape, per_sub):
    lane = lax.broadcasted_iota(jnp.int32, shape, 1)
    return (lane % SUB) * per_sub + lane // SUB


def one_hot(pos):
    place = row_positions(pos.shape, pos.shape[1] // SUB)
    hit = pos.astype(jnp.int32) == place
    return hit.astype(jnp.float32).astype(jnp.bfloat16)


def sort_kernel(arrived, sorted_rows, ahead, behind, places, plain):
    rows = sorted_rows.shape[0]
    group = rows // SUB
    width = arrived.shape[1]
    pieces = sorted_rows.shape[1] // width
    gather = spread_index(rows, turned=True)
    for q in range(SUB):
        part = as_bf16(matmul(gather, arrived[rows * q : rows * q + rows]))
        for k in range(pieces + 1):
            plain[group * q : group * q + group, width * k : width * k + width] = part[
                group * k : group * k + group
            ]
    pos = plain[:, width * pieces : width * pieces + LANES].astype(jnp.float32)
    places[...] = pos
    lane = lax.broadcasted_iota(jnp.int32, pos.shape, 1)
    edge = jnp.where(lane < SUB, lane + rows - 3, lane - SUB)
    edge = jnp.where((lane % SUB < 3) & (lane < 2 * SUB), edge, -1)
    hit = (pos.astype(jnp.int32) == edge).astype(jnp.float32).astype(jnp.bfloat16)
    data = plain[:, : width * pieces]
    ends = as_bf16(over_rows(hit, data))
    ahead[...] = ends[:SUB]
    behind[...] = ends[SUB : 2 * SUB]
    sorted_rows[...] = as_bf16(over_rows(one_hot(pos), data))


def inner_kernel(
    rows_in,
    conv_weight,
    conv_bias,
    weight,
    x_project,
    dt_project,
    u_out,
    proj_out,
    edge_sums,
    weight_here,
    x_here,
    dt_here,
    extended,
    sems,
):
    parts = sems.shape[0] - 2
    width = weight.shape[1] // parts
    rows = rows_in.shape[0]
    taps = conv_weight.shape[1]
    reach = taps - 1
    slots = rows // SUB
    moves = []
    for k in range(parts):
        cols = pl.ds(k * width, width)
        moves.append((weight.at[:, cols], weight_here.at[:, cols]))
        if k == 0:
            moves.append((x_project, x_here))
    moves.append((dt_project, dt_here))
    copies = [
        pltpu.make_async_copy(here, there, sems.at[k]) for k, (here, there) in enumerate(moves)
    ]
    for copy in copies:
        copy.start()
    proj_out[...] = jnp.zeros_like(proj_out)
    row = sublane((SUB, width))
    for k in range(parts):
        cols = slice(k * width, k * width + width)
        if k == 0:
            copies[0].wait()
            copies[1].wait()
        else:
            copies[k + 1].wait()
        main = as_bf16(matmul(rows_in[...], weight_here[:, cols])).astype(jnp.float32)
        extended[SUB * reach : SUB * reach + rows] = main
        for i in range(reach):
            own = main[rows - SUB * (reach - i) : rows - SUB * (reach - i - 1)]
            extended[SUB * i : SUB * i + SUB] = jnp.where(row == 0, 0.0, pltpu.roll(own, 1, 0))
            own = main[SUB * i : SUB * i + SUB]
            base = SUB * (reach + slots + i)
            extended[base : base + SUB] = jnp.where(
                row == SUB - 1, 0.0, pltpu.roll(own, SUB - 1, 0)
            )
        for d in range(2):
            mixed = conv_bias[d : d + 1, cols]
            for tap in range(taps):
                base = SUB * (2 * reach - tap if d else tap)
                mixed = mixed + conv_weight[d, tap : tap + 1, cols] * extended[base : base + rows]
            edge = SUB * reach
            edge_sums[d, :, cols] = mixed[rows - edge :] if d else mixed[:edge]
            u = as_bf16(silu(mixed))
            u_out[d, :, cols] = u
            proj_out[d] += matmul(u, x_here[d, cols, :])
    copies[parts + 1].wait()


def sublane(shape):
    return lax.broadcasted_iota(jnp.int32, shape, 0)


def shift_sublanes(tile, count, reverse):
    return pltpu.roll(tile, SUB - count if reverse else count, 0)


def in_reach(count, reverse):
    row = sublane((SUB, LANES))
    return row < SUB - count if reverse else row >= count


def outside(total, reverse):
    for count in (1, 2, 4):
        moved = shift_sublanes(total, count, reverse)
        total = total + jnp.where(in_reach(count, reverse), moved, 0.0)
    return jnp.where(in_reach(1, reverse), shift_sublanes(total, 1, reverse), 0.0)


def tiles_of(array):
    return [array[SUB * t : SUB * t + SUB] for t in range(array.shape[0] // SUB)]


def in_order(count, reverse):
    return list(range(count))[::-1] if reverse else list(range(count))


def spread_columns(target, columns, first, count):
    row = lax.broadcasted_iota(jnp.int32, (2 * count, count * LANES), 0)
    at = lax.broadcasted_iota(jnp.int32, (2 * count, count * LANES), 1)
    repeat = (row % count == at // LANES).astype(jnp.float32).astype(jnp.bfloat16)
    parts = [part[:, first : first + count] for part in halves(columns)]
    wide = matmul(jnp.concatenate(parts, axis=1), repeat)
    for n in range(count):
        target[n] = wide[:, LANES * n : LANES * n + LANES]


def silu(v):
    half = 0.5 * v
    return half + half * jnp.tanh(half)


def halves(array):
    high = as_bf16(array)
    return high, as_bf16(array - high.astype(jnp.float32))


def paired(first, second):
    return as_bf16(jnp.concatenate([first, second], axis=0))


def sum_over_states(columns, first, states):
    rows = columns.shape[0]
    size = (columns.shape[1], PACK * states)
    col = lax.broadcasted_iota(jnp.int32, size, 0)
    at = lax.broadcasted_iota(jnp.int32, size, 1)
    repeat = (col == first + at // PACK).astype(jnp.float32).astype(jnp.bfloat16)
    size = (rows, PACK * states)
    row = lax.broadcasted_iota(jnp.int32, size, 0)
    at = lax.broadcasted_iota(jnp.int32, size, 1)
    own = row % PACK == at % PACK
    return [as_bf16(jnp.where(own, matmul(part, repeat), 0.0)) for part in halves(columns)]


def softplus(v):
    return jnp.maximum(v, 0.0) + jnp.log(1.0 + jnp.exp(-jnp.abs(v)))


def states_kernel(
    flags,
    proj_in,
    edge_sums,
    before,
    after,
    w_inner,
    conv_weight,
    x_project,
    dt_project,
    dt_bias,
    rates,
    u_in,
    u_result,
    proj_result,
    dt_result,
    payload_result,
    ends_result,
    span_result,
    u_out,
    proj_out,
    dt_out,
    payload,
    ends,
    span,
    b_wide,
    edge_rows,
    sems,
):
    copies = [
        pltpu.make_async_copy(here, there, sems.at[k])
        for k, (here, there) in enumerate(
            (
                (u_out, u_result),
                (proj_out, proj_result),
                (dt_out, dt_result),
                (payload.at[0], payload_result.at[0]),
                (payload.at[1], payload_result.at[1]),
            )
        )
    ]
    _, rows, channels = u_out.shape
    taps = conv_weight.shape[1]
    reach = taps - 1
    width = channels // 4
    states = rates.shape[1]
    rank = dt_project.shape[1]
    slots = rows // SUB
    tile = payload.shape[4]
    edge = SUB * reach
    edge_rows[:SUB] = before[...]
    edge_rows[SUB:] = after[...]
    row = sublane((SUB, width))
    projected = [jnp.zeros((edge, LANES), jnp.float32)] * 2
    inside = [slice(edge, rows), slice(0, rows - edge)]
    outermost = [slice(0, edge), slice(rows - edge, rows)]
    low = [as_bf16(proj_in[d, inside[d]][:, :rank]) for d in range(2)]
    for step in range(channels // width):
        cols = slice(step * width, step * width + width)
        for d in range(2):
            raw = matmul(low[d], dt_project[d, :, cols])
            dt_out[d, inside[d], cols] = softplus(raw + dt_bias[d : d + 1, cols])
        edges = as_bf16(matmul(edge_rows[...], w_inner[:, cols])).astype(jnp.float32)
        prior = edges[:SUB] * flags[0].astype(jnp.float32)
        later = edges[SUB:] * flags[1].astype(jnp.float32)
        for d in range(2):
            tiles = []
            for m in range(reach):
                if d:
                    terms = [(tap, later[m - tap : m - tap + 1]) for tap in range(m + 1)]
                else:
                    terms = [(tap, prior[m + tap : m + tap + 1]) for tap in range(reach - m)]
                extra = sum(conv_weight[d, tap : tap + 1, cols] * term for tap, term in terms)
                mixed = edge_sums[d, SUB * m : SUB * m + SUB, cols]
                tiles.append(mixed + jnp.where(row == (SUB - 1 if d else 0), extra, 0.0))
            u = as_bf16(silu(jnp.concatenate(tiles, axis=0)))
            first = rows - edge if d else 0
            u_out[d, first : first + edge, cols] = u
            projected[d] = projected[d] + matmul(u, x_project[d, cols, :])
    copies[0].start()
    for d in range(2):
        proj_out[d] = proj_in[d]
        first = rows - edge if d else 0
        proj_out[d, first : first + edge] = projected[d]
    copies[1].start()
    for d in range(2):
        spread_columns(b_wide.at[d], proj_out[d], rank, states)

    for d in range(2):
        low = as_bf16(projected[d][:, :rank])
        raw = matmul(low, dt_project[d])
        dt_out[d, outermost[d]] = softplus(raw + dt_bias[d : d + 1])
    copies[2].start()
    row = sublane((SUB, LANES))

    def state_block(block, carry, d):
        here = pl.ds(pl.multiple_of(block * LANES, LANES), LANES)
        group = block // (tile // LANES)
        within = pl.multiple_of((block - group * (tile // LANES)) * LANES, LANES)
        reverse = d == 1
        dt = dt_out[d, :, here]
        fed = tiles_of(dt * u_out[d, :, here].astype(jnp.float32))
        dt = tiles_of(dt)
        total = dt[0]
        for t in range(1, slots):
            total = total + dt[t]
        span[d, :, here] = total
        after_it = outside(total, not reverse)
        finals = []
        for n in range(states):
            rate = rates[d, n : n + 1, here]
            state = None
            for t in in_order(slots, reverse):
                new = fed[t] * b_wide[d, n, SUB * t : SUB * t + SUB]
                if state is not None:
                    new = jnp.exp2(dt[t] * rate) * state + new
                state = new
            ends[d, n, :, here] = state
            state = jnp.exp2(after_it * rate) * state
            finals.append(jnp.sum(state, axis=0, keepdims=True))
        whole = jnp.sum(total, axis=0, keepdims=True)
        for n in range(0, states, 2):
            out = jnp.where(row == 0, finals[n], finals[n + 1])
            out = jnp.where(row >= 2, whole, out)
            payload[d, n // 2, group, :, pl.ds(within, LANES)] = as_bf16(out[:4])
        return carry

    thirds = channels // LANES // 3
    for d in range(2):
        for part in range(3):
            body = functools.partial(state_block, d=d)
            lax.fori_loop(part * thirds, part * thirds + thirds, body, 0)
            cols = pl.ds(part * thirds * LANES, thirds * LANES)
            copies.append(
                pltpu.make_async_copy(
                    ends.at[d, :, :, cols],
                    ends_result.at[d, :, :, cols],
                    sems.at[5 + 3 * d + part],
                )
            )
            copies[-1].start()
        copies[3 + d].start()
    copies.append(pltpu.make_async_copy(span, span_result, sems.at[11]))
    copies[-1].start()
    for copy in copies:
        copy.wait()


def entry_kernel(ends, span, rates, entry):
    states = rates.shape[1]
    for at in range(0, span.shape[2], LANES):
        here = slice(at, at + LANES)
        for d in range(2):
            reverse = d == 1
            near = in_reach(1, reverse)
            for n in range(states):
                state = ends[d, n, :, here]
                keep = jnp.exp2(span[d, :, here] * rates[d, n : n + 1, here])
                for count in (1, 2, 4):
                    keep = jnp.where(in_reach(count, reverse), keep, 0.0)
                    state = state + keep * shift_sublanes(state, count, reverse)
                    if count < 4:
                        keep = keep * shift_sublanes(keep, count, reverse)
                entry[d, n, :, here] = jnp.where(near, shift_sublanes(state, 1, reverse), 0.0)


def relay_kernel(keep, payload, rates, entering):
    blocks = payload.shape[0]
    backward = keep[blocks]

    def block_step(i, state):
        at = jnp.where(backward == 1, blocks - 1 - i, i)
        state = state * keep[at].astype(jnp.float32)
        entering[at] = state.astype(jnp.bfloat16)
        row = payload[at].astype(jnp.float32)
        return jnp.exp2(rates[...] * row[2:3]) * state + row[0:2]

    lax.fori_loop(0, blocks, block_step, jnp.zeros(rates.shape, jnp.float32), unroll=16)


def outputs_kernel(
    entering,
    entry,
    dt_in,
    u_in,
    proj,
    rates,
    skip_gain,
    places,
    out,
    left,
    b_wide,
    placed,
):
    step = pl.program_id(0)
    states = rates.shape[1]
    _, rows, channels = dt_in.shape
    slots = rows // SUB
    rank = proj.shape[2] - 2 * states
    tile = entering.shape[4]

    @pl.when(step == 0)
    def _():
        for d in range(2):
            spread_columns(b_wide.at[d], proj[d], rank, states)
            parts = sum_over_states(proj[d], rank + states, states)
            for k in range(slots // 2):
                for i, part in enumerate(parts):
                    left[d, k, PACK * i : PACK * i + PACK] = part[PACK * k : PACK * k + PACK]

    def swept(at, d):
        here = slice(at * LANES, at * LANES + LANES)
        block = step * (channels // LANES) + at
        group = block // (tile // LANES)
        within = pl.multiple_of((block - group * (tile // LANES)) * LANES, LANES)
        reverse = d == 1
        total = dt_in[d, :SUB, here]
        for t in range(1, slots):
            total = total + dt_in[d, SUB * t : SUB * t + SUB, here]
        ahead = outside(total, reverse)
        state = []
        for n in range(states):
            pair = entering[d, n // 2, group, :, pl.ds(within, LANES)].astype(jnp.float32)
            carried = jnp.exp2(ahead * rates[d, n : n + 1, here]) * pair[n % 2 : n % 2 + 1]
            state.append(carried + entry[d, n, :, here])
        sums = [None] * (slots // 2)
        for k in in_order(slots // 2, reverse):
            right = []
            two = slice(PACK * k, PACK * k + PACK)
            u = u_in[d, two, here].astype(jnp.float32)
            dt = dt_in[d, two, here]
            fed = tiles_of(dt * u)
            dt = tiles_of(dt)
            for n in range(states):
                rate = rates[d, n : n + 1, here]
                both = []
                for t in in_order(2, reverse):
                    first = PACK * k + SUB * t
                    new = fed[t] * b_wide[d, n, first : first + SUB]
                    state[n] = jnp.exp2(dt[t] * rate) * state[n] + new
                    both.append(state[n])
                right.append(paired(*(both[::-1] if reverse else both)))
            part = matmul(left[d, k], jnp.concatenate(right, axis=0))
            sums[k] = part[:PACK] + part[PACK:] + skip_gain[d : d + 1, here] * u
        return jnp.concatenate(sums, axis=0)

    pick = one_hot(places[...])
    for at in range(channels // LANES):
        total = swept(at, 0) + swept(at, 1)
        start = pl.multiple_of(step * channels + at * LANES, LANES)
        placed[:, pl.ds(start, LANES)] = as_bf16(matmul(pick, as_bf16(total)))

    @pl.when(step == pl.num_programs(0) - 1)
    def _():
        chunked([placed[:, tile * k : tile * k + tile] for k in range(SUB)], out)


def gate_kernel(returned, gate, out):
    rows = out.shape[0]
    group = rows // SUB
    width = returned.shape[1]
    gather = spread_index(rows, turned=True)
    for q in range(SUB):
        part = matmul(gather, returned[rows * q : rows * q + rows])
        here = slice(group * q, group * q + group)
        for k in range(SUB):
            cols = slice(width * k, width * k + width)
            out[here, cols] = as_bf16(part[group * k : group * k + group] * gate[here, cols])


def limits(mebibytes):
    return pltpu.CompilerParams(vmem_limit_bytes=mebibytes * 1024 * 1024)


def in_vmem(array):
    return pltpu.with_memory_space_constraint(array, pltpu.VMEM)


def in_hbm(array):
    return pltpu.with_memory_space_constraint(array, pltpu.HBM)


def on_chip(kernel, name, mebibytes, results, *operands, scalars=0, scratch=()):
    places = [pltpu.SMEM] * scalars + [pltpu.VMEM] * (len(operands) - scalars)
    one = pl.BlockSpec(memory_space=pltpu.VMEM)
    return pl.pallas_call(
        kernel,
        out_shape=results,
        in_specs=[pl.BlockSpec(memory_space=place) for place in places],
        out_specs=tuple(one for _ in results) if isinstance(results, tuple) else one,
        scratch_shapes=list(scratch),
        compiler_params=limits(mebibytes),
        name=name,
    )(
        *(
            in_vmem(operand) if place is pltpu.VMEM else operand
            for operand, place in zip(operands, places)
        )
    )


def local(
    tile_embed,
    destination,
    slide_lengths,
    w_inner,
    w_gate,
    conv_weight,
    conv_bias,
    x_project,
    dt_project,
    dt_bias,
    decay,
    skip_gain,
):
    f32, bf16 = jnp.float32, jnp.bfloat16
    shards = lax.axis_size(AXES)
    me = lax.axis_index(AXES)
    rows, model = tile_embed.shape
    width = w_inner.shape[1]
    states = decay.shape[1]
    rank = dt_project.shape[1]
    taps = conv_weight.shape[1]
    tile = 3 * LANES
    groups = width // tile
    owner_states = 2 * groups * states // shards
    state_groups = states // owner_states
    slots = rows // SUB

    blocks = jnp.arange(shards, dtype=jnp.int32)
    slide = jnp.arange(slide_lengths.shape[0], dtype=jnp.int32)
    ends = jnp.sum(jnp.where(slide[:, None] <= slide[None, :], slide_lengths[:, None], 0), axis=0)
    starts = ends - slide_lengths
    opens = jnp.any(blocks[:, None] * rows == starts[None, :], axis=1)
    closes = jnp.any((blocks[:, None] + 1) * rows == ends[None, :], axis=1)
    mine = blocks == me
    flags = jnp.stack([~jnp.any(opens & mine), ~jnp.any(closes & mine)]).astype(jnp.int32)
    owner_dir = me // (state_groups * groups)
    owner_group = (me // groups) % state_groups
    owner_tile = me % groups
    keep = jnp.where(owner_dir == 1, ~closes, ~opens).astype(jnp.int32)
    keep = jnp.concatenate([keep, jnp.full((SUB,), owner_dir, jnp.int32)])
    rates = decay * (-LOG2E)
    owner_rates = lax.dynamic_slice(
        rates, (owner_dir, owner_group * owner_states, owner_tile * tile), (1, owner_states, tile)
    )[0]

    piece = 2 * LANES
    sent = pl.pallas_call(
        pack_kernel,
        out_shape=pltpu.VMEM((SUB * rows, piece), bf16),
        compiler_params=limits(3),
        name="pack",
    )(in_hbm(tile_embed), in_hbm(destination[None, :]))
    arrived = lax.all_to_all(
        sent.reshape(rows, SUB, piece), AXES, split_axis=0, concat_axis=0, tiled=True
    ).reshape(SUB * rows, piece)
    gate = jax.nn.silu(jnp.dot(tile_embed, w_gate, preferred_element_type=f32))

    block_rows, ahead, behind, places = on_chip(
        sort_kernel,
        "sort_rows",
        4,
        (
            pltpu.VMEM((rows, model), bf16),
            pltpu.VMEM((SUB, model), bf16),
            pltpu.VMEM((SUB, model), bf16),
            pltpu.HBM((rows, LANES), f32),
        ),
        arrived,
        scratch=[pltpu.VMEM((rows, model + piece), bf16)],
    )
    before = lax.ppermute(ahead, AXES, [(i, i + 1) for i in range(shards - 1)])
    after = lax.ppermute(behind, AXES, [(i + 1, i) for i in range(shards - 1)])
    hbm_spec = pl.BlockSpec(memory_space=pltpu.HBM)
    vmem_spec = pl.BlockSpec(memory_space=pltpu.VMEM)
    weights = (w_inner, x_project, dt_project)
    edge = SUB * (taps - 1)
    results = (
        pltpu.VMEM((2, rows, width), bf16),
        pltpu.VMEM((2, rows, LANES), f32),
        pltpu.VMEM((2, edge, width), f32),
        *(pltpu.VMEM(w.shape, w.dtype) for w in weights),
    )
    u, proj, edge_sums, w_inner, x_project, dt_project = pl.pallas_call(
        inner_kernel,
        out_shape=results,
        in_specs=[vmem_spec] * 3 + [hbm_spec] * 3,
        out_specs=(vmem_spec,) * len(results),
        scratch_shapes=[
            pltpu.VMEM((rows + 2 * edge, width // 4), f32),
            pltpu.SemaphoreType.DMA((6,)),
        ],
        compiler_params=limits(4),
        name="inner",
    )(
        *(in_vmem(operand) for operand in (block_rows, conv_weight, conv_bias)),
        *(in_hbm(w) for w in weights),
    )

    operands = (
        proj, edge_sums, before, after, w_inner, conv_weight, x_project, dt_project, dt_bias, rates, u,
    )
    on_chip_results = [
        pltpu.VMEM((2, rows, LANES), f32),
        pltpu.VMEM((2, rows, width), f32),
        pltpu.VMEM((2, state_groups, groups, 4, tile), bf16),
        pltpu.VMEM((2, states, SUB, width), f32),
        pltpu.VMEM((2, SUB, width), f32),
        pltpu.VMEM((2, states, rows, LANES), f32),
    ]
    u, proj, dt, payload, ends, span, _ = pl.pallas_call(
        states_kernel,
        out_shape=(
            pltpu.HBM((2, rows, width), bf16),
            pltpu.HBM((2, rows, LANES), f32),
            pltpu.HBM((2, rows, width), f32),
            pltpu.HBM((2, state_groups, groups, 4, tile), bf16),
            pltpu.HBM((2, states, SUB, width), f32),
            pltpu.HBM((2, SUB, width), f32),
            pltpu.VMEM((2, rows, width), bf16),
        ),
        in_specs=[pl.BlockSpec(memory_space=pltpu.SMEM)] + [vmem_spec] * len(operands),
        out_specs=(hbm_spec,) * 6 + (vmem_spec,),
        input_output_aliases={len(operands): 6},
        scratch_shapes=on_chip_results
        + [
            pltpu.VMEM((2 * SUB, model), bf16),
            pltpu.SemaphoreType.DMA((12,)),
        ],
        compiler_params=limits(14),
        name="block_states",
    )(flags, *(in_vmem(operand) for operand in operands))

    part = 4 * LANES
    shared = lax.all_to_all(
        payload.reshape(shards, 4, tile), AXES, split_axis=0, concat_axis=0, tiled=True
    )
    entry = pl.pallas_call(
        entry_kernel,
        out_shape=pltpu.HBM((2, states, SUB, width), f32),
        grid=(width // part,),
        in_specs=[
            pl.BlockSpec((2, states, SUB, part), lambda i: (0, 0, 0, i)),
            pl.BlockSpec((2, SUB, part), lambda i: (0, 0, i)),
            pl.BlockSpec((2, states, part), lambda i: (0, 0, i)),
        ],
        out_specs=pl.BlockSpec((2, states, SUB, part), lambda i: (0, 0, 0, i)),
        compiler_params=limits(3),
        name="entries",
    )(in_hbm(ends), in_hbm(span), rates)
    shared, entry = lax.optimization_barrier((shared, entry))
    entering = on_chip(
        relay_kernel,
        "relay",
        2,
        pltpu.VMEM((shards, owner_states, tile), bf16),
        keep, shared, owner_rates,
        scalars=1,
    )
    entering = lax.all_to_all(entering, AXES, split_axis=0, concat_axis=0, tiled=True)
    entering = entering.reshape(2, state_groups, groups, owner_states, tile)

    totals = pl.pallas_call(
        outputs_kernel,
        out_shape=pltpu.HBM((SUB * rows, tile), bf16),
        grid=(width // part,),
        in_specs=[
            vmem_spec,
            pl.BlockSpec((2, states, SUB, part), lambda i: (0, 0, 0, i)),
            pl.BlockSpec((2, rows, part), lambda i: (0, 0, i)),
            pl.BlockSpec((2, rows, part), lambda i: (0, 0, i)),
            pl.BlockSpec((2, rows, LANES), lambda i: (0, 0, 0)),
            pl.BlockSpec((2, states, part), lambda i: (0, 0, i)),
            pl.BlockSpec((2, part), lambda i: (0, i)),
            pl.BlockSpec((rows, LANES), lambda i: (0, 0)),
        ],
        out_specs=pl.BlockSpec((SUB * rows, tile), lambda i: (0, 0)),
        scratch_shapes=[
            pltpu.VMEM((2, slots // 2, 2 * PACK, PACK * states), bf16),
            pltpu.VMEM((2, states, rows, LANES), f32),
            pltpu.VMEM((rows, width), bf16),
        ],
        compiler_params=limits(12),
        name="block_outputs",
    )(
        in_vmem(entering),
        *(in_hbm(array) for array in (entry, dt, u, proj)),
        rates,
        skip_gain,
        in_hbm(places),
    )

    returned = lax.all_to_all(
        totals.reshape(rows, SUB, tile), AXES, split_axis=0, concat_axis=0, tiled=True
    ).reshape(SUB * rows, tile)
    return pl.pallas_call(
        gate_kernel,
        out_shape=jax.ShapeDtypeStruct((rows, width), bf16),
        compiler_params=limits(5),
        name="gated",
    )(in_vmem(returned), gate)


def solution(mesh):
    placed = (P(AXES, None), P(AXES)) + (P(),) * 10
    return jax.shard_map(
        local, mesh=mesh, in_specs=placed, out_specs=P(AXES, None), check_vma=False
    )
```

```python
import functools

import jax
import jax.numpy as jnp
from jax import lax
from jax.experimental import pallas as pl
from jax.experimental.pallas import tpu as pltpu
from jax.sharding import PartitionSpec as P

AXES = ("seq", "slide")
SUB = 8
LANES = 128
PACK = 16
LOG2E = 1.4426950408889634


def spread_index(rows, turned=False):
    shape = (rows, rows)
    row = lax.broadcasted_iota(jnp.int32, shape, 1 if turned else 0)
    col = lax.broadcasted_iota(jnp.int32, shape, 0 if turned else 1)
    group = rows // SUB
    hit = (row // SUB == col % group) & (row % SUB == col // group)
    return hit.astype(jnp.float32).astype(jnp.bfloat16)


def as_bf16(product):
    return product.astype(jnp.bfloat16)


def matmul(left, right):
    return jnp.dot(left, right, preferred_element_type=jnp.float32)


def over_rows(left, right):
    return lax.dot_general(
        left, right, (((0,), (0,)), ((), ())), preferred_element_type=jnp.float32
    )


def chunked(pieces, out):
    rows = pieces[0].shape[0]
    group = rows // SUB
    spread = spread_index(rows)
    blank = [jnp.zeros_like(pieces[0])] * (SUB - len(pieces))
    for q in range(SUB):
        part = [piece[group * q : group * q + group] for piece in list(pieces) + blank]
        out[rows * q : rows * q + rows] = as_bf16(matmul(spread, jnp.concatenate(part, axis=0)))


def pack_kernel(embed, destination, out):
    rows = embed.shape[0]
    width = out.shape[1]
    pieces = [embed[:, at : at + width] for at in range(0, embed.shape[1], width)]
    row = lax.broadcasted_iota(jnp.int32, (rows, rows), 0)
    col = lax.broadcasted_iota(jnp.int32, (rows, rows), 1)
    offset = jnp.where(row == col, destination[...] - rows * col, 0)
    offset = as_bf16(offset.astype(jnp.float32))
    pieces.append(as_bf16(matmul(offset, jnp.ones((rows, width), jnp.bfloat16))))
    chunked(pieces, out)


def row_positions(shape, per_sub):
    lane = lax.broadcasted_iota(jnp.int32, shape, 1)
    return (lane % SUB) * per_sub + lane // SUB


def one_hot(pos):
    place = row_positions(pos.shape, pos.shape[1] // SUB)
    hit = pos.astype(jnp.int32) == place
    return hit.astype(jnp.float32).astype(jnp.bfloat16)


def edges_kernel(arrived, plain, first_out, second_out):
    rows = plain.shape[0]
    group = rows // SUB
    width = arrived.shape[1]
    pieces = plain.shape[1] // width
    gather = spread_index(rows, turned=True)
    for q in range(SUB):
        part = as_bf16(matmul(gather, arrived[rows * q : rows * q + rows]))
        for k in range(pieces):
            plain[group * q : group * q + group, width * k : width * k + width] = part[
                group * k : group * k + group
            ]
    model = width * (pieces - 1)
    pos = plain[:, model : model + LANES].astype(jnp.float32)
    lane = lax.broadcasted_iota(jnp.int32, pos.shape, 1)
    ahead = lane + rows - 3
    behind = lane % SUB
    odd = lax.axis_index(AXES[1]) % 2
    early = lane < SUB
    edge = jnp.where(early == (odd == 0), jnp.where(early, ahead, ahead - SUB), behind)
    edge = jnp.where((lane % SUB < 3) & (lane < 2 * SUB), edge, -1)
    hit = (pos.astype(jnp.int32) == edge).astype(jnp.float32).astype(jnp.bfloat16)
    ends = as_bf16(over_rows(hit, plain[:, :model]))
    first_out[...] = ends[:SUB]
    second_out[...] = ends[SUB : 2 * SUB]


def inner_kernel(
    plain,
    conv_weight,
    conv_bias,
    weight,
    x_project,
    dt_project,
    u_out,
    proj_out,
    edge_sums,
    weight_here,
    x_here,
    dt_here,
    places_result,
    rows_in,
    places,
    extended,
    sems,
):
    parts = sems.shape[0] - 3
    width = weight.shape[1] // parts
    rows, model = rows_in.shape
    taps = conv_weight.shape[1]
    reach = taps - 1
    slots = rows // SUB
    moves = []
    for k in range(parts):
        cols = pl.ds(k * width, width)
        moves.append((weight.at[:, cols], weight_here.at[:, cols]))
        if k == 0:
            moves.append((x_project, x_here))
    moves.append((dt_project, dt_here))
    copies = [
        pltpu.make_async_copy(here, there, sems.at[k]) for k, (here, there) in enumerate(moves)
    ]
    for copy in copies:
        copy.start()
    pos = plain[:, model : model + LANES].astype(jnp.float32)
    places[...] = pos
    copies.append(pltpu.make_async_copy(places, places_result, sems.at[parts + 2]))
    copies[-1].start()
    rows_in[...] = as_bf16(over_rows(one_hot(pos), plain[:, :model]))
    proj_out[...] = jnp.zeros_like(proj_out)
    row = sublane((SUB, width))
    for k in range(parts):
        cols = slice(k * width, k * width + width)
        if k == 0:
            copies[0].wait()
            copies[1].wait()
        else:
            copies[k + 1].wait()
        main = as_bf16(matmul(rows_in[...], weight_here[:, cols])).astype(jnp.float32)
        extended[SUB * reach : SUB * reach + rows] = main
        for i in range(reach):
            own = main[rows - SUB * (reach - i) : rows - SUB * (reach - i - 1)]
            extended[SUB * i : SUB * i + SUB] = jnp.where(row == 0, 0.0, pltpu.roll(own, 1, 0))
            own = main[SUB * i : SUB * i + SUB]
            base = SUB * (reach + slots + i)
            extended[base : base + SUB] = jnp.where(
                row == SUB - 1, 0.0, pltpu.roll(own, SUB - 1, 0)
            )
        for d in range(2):
            mixed = conv_bias[d : d + 1, cols]
            for tap in range(taps):
                base = SUB * (2 * reach - tap if d else tap)
                mixed = mixed + conv_weight[d, tap : tap + 1, cols] * extended[base : base + rows]
            edge = SUB * reach
            edge_sums[d, :, cols] = mixed[rows - edge :] if d else mixed[:edge]
            u = as_bf16(silu(mixed))
            u_out[d, :, cols] = u
            proj_out[d] += matmul(u, x_here[d, cols, :])
    copies[parts + 1].wait()
    copies[parts + 2].wait()


def sublane(shape):
    return lax.broadcasted_iota(jnp.int32, shape, 0)


def shift_sublanes(tile, count, reverse):
    return pltpu.roll(tile, SUB - count if reverse else count, 0)


def in_reach(count, reverse):
    row = sublane((SUB, LANES))
    return row < SUB - count if reverse else row >= count


def outside(total, reverse):
    for count in (1, 2, 4):
        moved = shift_sublanes(total, count, reverse)
        total = total + jnp.where(in_reach(count, reverse), moved, 0.0)
    return jnp.where(in_reach(1, reverse), shift_sublanes(total, 1, reverse), 0.0)


def tiles_of(array):
    return [array[SUB * t : SUB * t + SUB] for t in range(array.shape[0] // SUB)]


def in_order(count, reverse):
    return list(range(count))[::-1] if reverse else list(range(count))


def spread_columns(target, columns, first, count):
    row = lax.broadcasted_iota(jnp.int32, (2 * count, count * LANES), 0)
    at = lax.broadcasted_iota(jnp.int32, (2 * count, count * LANES), 1)
    repeat = (row % count == at // LANES).astype(jnp.float32).astype(jnp.bfloat16)
    parts = [part[:, first : first + count] for part in halves(columns)]
    wide = matmul(jnp.concatenate(parts, axis=1), repeat)
    for n in range(count):
        target[n] = wide[:, LANES * n : LANES * n + LANES]


def silu(v):
    half = 0.5 * v
    return half + half * jnp.tanh(half)


def halves(array):
    high = as_bf16(array)
    return high, as_bf16(array - high.astype(jnp.float32))


def paired(first, second):
    return as_bf16(jnp.concatenate([first, second], axis=0))


def sum_over_states(columns, first, states):
    rows = columns.shape[0]
    size = (columns.shape[1], PACK * states)
    col = lax.broadcasted_iota(jnp.int32, size, 0)
    at = lax.broadcasted_iota(jnp.int32, size, 1)
    repeat = (col == first + at // PACK).astype(jnp.float32).astype(jnp.bfloat16)
    size = (rows, PACK * states)
    row = lax.broadcasted_iota(jnp.int32, size, 0)
    at = lax.broadcasted_iota(jnp.int32, size, 1)
    own = row % PACK == at % PACK
    return [as_bf16(jnp.where(own, matmul(part, repeat), 0.0)) for part in halves(columns)]


def softplus(v):
    return jnp.maximum(v, 0.0) + jnp.log(1.0 + jnp.exp(-jnp.abs(v)))


def states_kernel(
    flags,
    proj_in,
    edge_sums,
    first_in,
    second_in,
    w_inner,
    conv_weight,
    x_project,
    dt_project,
    dt_bias,
    rates,
    u_in,
    u_result,
    proj_result,
    dt_result,
    payload_result,
    ends_result,
    span_result,
    u_out,
    proj_out,
    dt_out,
    payload,
    ends,
    span,
    b_wide,
    edge_rows,
    sems,
):
    copies = [
        pltpu.make_async_copy(here, there, sems.at[k])
        for k, (here, there) in enumerate(
            (
                (u_out, u_result),
                (proj_out, proj_result),
                (dt_out, dt_result),
                (payload.at[0], payload_result.at[0]),
                (payload.at[1], payload_result.at[1]),
            )
        )
    ]
    _, rows, channels = u_out.shape
    taps = conv_weight.shape[1]
    reach = taps - 1
    width = channels // 4
    states = rates.shape[1]
    rank = dt_project.shape[1]
    slots = rows // SUB
    tile = payload.shape[4]
    edge = SUB * reach
    even = flags[2] == 0
    edge_rows[:SUB] = jnp.where(even, second_in[...], first_in[...])
    edge_rows[SUB:] = jnp.where(even, first_in[...], second_in[...])
    row = sublane((SUB, width))
    projected = [jnp.zeros((edge, LANES), jnp.float32)] * 2
    inside = [slice(edge, rows), slice(0, rows - edge)]
    outermost = [slice(0, edge), slice(rows - edge, rows)]
    low = [as_bf16(proj_in[d, inside[d]][:, :rank]) for d in range(2)]
    for step in range(channels // width):
        cols = slice(step * width, step * width + width)
        for d in range(2):
            raw = matmul(low[d], dt_project[d, :, cols])
            dt_out[d, inside[d], cols] = softplus(raw + dt_bias[d : d + 1, cols])
        edges = as_bf16(matmul(edge_rows[...], w_inner[:, cols])).astype(jnp.float32)
        prior = edges[:SUB] * flags[0].astype(jnp.float32)
        later = edges[SUB:] * flags[1].astype(jnp.float32)
        for d in range(2):
            tiles = []
            for m in range(reach):
                if d:
                    terms = [(tap, later[m - tap : m - tap + 1]) for tap in range(m + 1)]
                else:
                    terms = [(tap, prior[m + tap : m + tap + 1]) for tap in range(reach - m)]
                extra = sum(conv_weight[d, tap : tap + 1, cols] * term for tap, term in terms)
                mixed = edge_sums[d, SUB * m : SUB * m + SUB, cols]
                tiles.append(mixed + jnp.where(row == (SUB - 1 if d else 0), extra, 0.0))
            u = as_bf16(silu(jnp.concatenate(tiles, axis=0)))
            first = rows - edge if d else 0
            u_out[d, first : first + edge, cols] = u
            projected[d] = projected[d] + matmul(u, x_project[d, cols, :])
    copies[0].start()
    for d in range(2):
        proj_out[d] = proj_in[d]
        first = rows - edge if d else 0
        proj_out[d, first : first + edge] = projected[d]
    copies[1].start()
    for d in range(2):
        spread_columns(b_wide.at[d], proj_out[d], rank, states)

    for d in range(2):
        low = as_bf16(projected[d][:, :rank])
        raw = matmul(low, dt_project[d])
        dt_out[d, outermost[d]] = softplus(raw + dt_bias[d : d + 1])
    copies[2].start()
    row = sublane((SUB, LANES))

    def state_block(block, carry, d):
        here = pl.ds(pl.multiple_of(block * LANES, LANES), LANES)
        group = block // (tile // LANES)
        within = pl.multiple_of((block - group * (tile // LANES)) * LANES, LANES)
        reverse = d == 1
        dt = dt_out[d, :, here]
        fed = tiles_of(dt * u_out[d, :, here].astype(jnp.float32))
        dt = tiles_of(dt)
        total = dt[0]
        for t in range(1, slots):
            total = total + dt[t]
        span[d, :, here] = total
        after_it = outside(total, not reverse)
        finals = []
        for n in range(states):
            rate = rates[d, n : n + 1, here]
            state = None
            for t in in_order(slots, reverse):
                new = fed[t] * b_wide[d, n, SUB * t : SUB * t + SUB]
                if state is not None:
                    new = jnp.exp2(dt[t] * rate) * state + new
                state = new
            ends[d, n, :, here] = state
            state = jnp.exp2(after_it * rate) * state
            finals.append(jnp.sum(state, axis=0, keepdims=True))
        whole = jnp.sum(total, axis=0, keepdims=True)
        for n in range(0, states, 2):
            out = jnp.where(row == 0, finals[n], finals[n + 1])
            out = jnp.where(row >= 2, whole, out)
            payload[d, n // 2, group, :, pl.ds(within, LANES)] = as_bf16(out[:4])
        return carry

    thirds = channels // LANES // 3
    for d in range(2):
        for part in range(3):
            body = functools.partial(state_block, d=d)
            lax.fori_loop(part * thirds, part * thirds + thirds, body, 0)
            cols = pl.ds(part * thirds * LANES, thirds * LANES)
            copies.append(
                pltpu.make_async_copy(
                    ends.at[d, :, :, cols],
                    ends_result.at[d, :, :, cols],
                    sems.at[5 + 3 * d + part],
                )
            )
            copies[-1].start()
        copies[3 + d].start()
    copies.append(pltpu.make_async_copy(span, span_result, sems.at[11]))
    copies[-1].start()
    for copy in copies:
        copy.wait()


def entry_kernel(ends, span, rates, entry):
    states = rates.shape[1]
    for at in range(0, span.shape[2], LANES):
        here = slice(at, at + LANES)
        for d in range(2):
            reverse = d == 1
            near = in_reach(1, reverse)
            for n in range(states):
                state = ends[d, n, :, here]
                keep = jnp.exp2(span[d, :, here] * rates[d, n : n + 1, here])
                for count in (1, 2, 4):
                    keep = jnp.where(in_reach(count, reverse), keep, 0.0)
                    state = state + keep * shift_sublanes(state, count, reverse)
                    if count < 4:
                        keep = keep * shift_sublanes(keep, count, reverse)
                entry[d, n, :, here] = jnp.where(near, shift_sublanes(state, 1, reverse), 0.0)


def relay_kernel(keep, payload, rates, entering):
    blocks = payload.shape[0]
    backward = keep[blocks]

    def block_step(i, state):
        at = jnp.where(backward == 1, blocks - 1 - i, i)
        state = state * keep[at].astype(jnp.float32)
        entering[at] = state.astype(jnp.bfloat16)
        row = payload[at].astype(jnp.float32)
        return jnp.exp2(rates[...] * row[2:3]) * state + row[0:2]

    lax.fori_loop(0, blocks, block_step, jnp.zeros(rates.shape, jnp.float32), unroll=16)


def outputs_kernel(
    entering,
    entry,
    dt_in,
    u_in,
    proj,
    rates,
    skip_gain,
    places,
    out,
    left,
    b_wide,
    placed,
):
    step = pl.program_id(0)
    states = rates.shape[1]
    _, rows, channels = dt_in.shape
    slots = rows // SUB
    rank = proj.shape[2] - 2 * states
    tile = entering.shape[4]

    @pl.when(step == 0)
    def _():
        for d in range(2):
            spread_columns(b_wide.at[d], proj[d], rank, states)
            parts = sum_over_states(proj[d], rank + states, states)
            for k in range(slots // 2):
                for i, part in enumerate(parts):
                    left[d, k, PACK * i : PACK * i + PACK] = part[PACK * k : PACK * k + PACK]

    def swept(at, d):
        here = slice(at * LANES, at * LANES + LANES)
        block = step * (channels // LANES) + at
        group = block // (tile // LANES)
        within = pl.multiple_of((block - group * (tile // LANES)) * LANES, LANES)
        reverse = d == 1
        total = dt_in[d, :SUB, here]
        for t in range(1, slots):
            total = total + dt_in[d, SUB * t : SUB * t + SUB, here]
        ahead = outside(total, reverse)
        state = []
        for n in range(states):
            pair = entering[d, n // 2, group, :, pl.ds(within, LANES)].astype(jnp.float32)
            carried = jnp.exp2(ahead * rates[d, n : n + 1, here]) * pair[n % 2 : n % 2 + 1]
            state.append(carried + entry[d, n, :, here])
        sums = [None] * (slots // 2)
        for k in in_order(slots // 2, reverse):
            right = []
            two = slice(PACK * k, PACK * k + PACK)
            u = u_in[d, two, here].astype(jnp.float32)
            dt = dt_in[d, two, here]
            fed = tiles_of(dt * u)
            dt = tiles_of(dt)
            for n in range(states):
                rate = rates[d, n : n + 1, here]
                both = []
                for t in in_order(2, reverse):
                    first = PACK * k + SUB * t
                    new = fed[t] * b_wide[d, n, first : first + SUB]
                    state[n] = jnp.exp2(dt[t] * rate) * state[n] + new
                    both.append(state[n])
                right.append(paired(*(both[::-1] if reverse else both)))
            part = matmul(left[d, k], jnp.concatenate(right, axis=0))
            sums[k] = part[:PACK] + part[PACK:] + skip_gain[d : d + 1, here] * u
        return jnp.concatenate(sums, axis=0)

    pick = one_hot(places[...])
    for at in range(channels // LANES):
        total = swept(at, 0) + swept(at, 1)
        start = pl.multiple_of(step * channels + at * LANES, LANES)
        placed[:, pl.ds(start, LANES)] = as_bf16(matmul(pick, as_bf16(total)))

    @pl.when(step == pl.num_programs(0) - 1)
    def _():
        chunked([placed[:, tile * k : tile * k + tile] for k in range(SUB)], out)


def gate_kernel(returned, gate, out):
    rows = out.shape[0]
    group = rows // SUB
    width = returned.shape[1]
    gather = spread_index(rows, turned=True)
    for q in range(SUB):
        part = matmul(gather, returned[rows * q : rows * q + rows])
        here = slice(group * q, group * q + group)
        for k in range(SUB):
            cols = slice(width * k, width * k + width)
            out[here, cols] = as_bf16(part[group * k : group * k + group] * gate[here, cols])


def limits(mebibytes):
    return pltpu.CompilerParams(vmem_limit_bytes=mebibytes * 1024 * 1024)


def in_vmem(array):
    return pltpu.with_memory_space_constraint(array, pltpu.VMEM)


def in_hbm(array):
    return pltpu.with_memory_space_constraint(array, pltpu.HBM)


def on_chip(kernel, name, mebibytes, results, *operands, scalars=0, scratch=()):
    places = [pltpu.SMEM] * scalars + [pltpu.VMEM] * (len(operands) - scalars)
    one = pl.BlockSpec(memory_space=pltpu.VMEM)
    return pl.pallas_call(
        kernel,
        out_shape=results,
        in_specs=[pl.BlockSpec(memory_space=place) for place in places],
        out_specs=tuple(one for _ in results) if isinstance(results, tuple) else one,
        scratch_shapes=list(scratch),
        compiler_params=limits(mebibytes),
        name=name,
    )(
        *(
            in_vmem(operand) if place is pltpu.VMEM else operand
            for operand, place in zip(operands, places)
        )
    )


def local(
    tile_embed,
    destination,
    slide_lengths,
    w_inner,
    w_gate,
    conv_weight,
    conv_bias,
    x_project,
    dt_project,
    dt_bias,
    decay,
    skip_gain,
):
    f32, bf16 = jnp.float32, jnp.bfloat16
    shards = lax.axis_size(AXES)
    me = lax.axis_index(AXES)
    rows, model = tile_embed.shape
    width = w_inner.shape[1]
    states = decay.shape[1]
    rank = dt_project.shape[1]
    taps = conv_weight.shape[1]
    tile = 3 * LANES
    groups = width // tile
    owner_states = 2 * groups * states // shards
    state_groups = states // owner_states
    slots = rows // SUB

    blocks = jnp.arange(shards, dtype=jnp.int32)
    slide = jnp.arange(slide_lengths.shape[0], dtype=jnp.int32)
    ends = jnp.sum(jnp.where(slide[:, None] <= slide[None, :], slide_lengths[:, None], 0), axis=0)
    starts = ends - slide_lengths
    opens = jnp.any(blocks[:, None] * rows == starts[None, :], axis=1)
    closes = jnp.any((blocks[:, None] + 1) * rows == ends[None, :], axis=1)
    mine = blocks == me
    flags = jnp.stack([~jnp.any(opens & mine), ~jnp.any(closes & mine), me % 2 == 1]).astype(jnp.int32)
    owner_dir = me // (state_groups * groups)
    owner_group = (me // groups) % state_groups
    owner_tile = me % groups
    keep = jnp.where(owner_dir == 1, ~closes, ~opens).astype(jnp.int32)
    keep = jnp.concatenate([keep, jnp.full((SUB,), owner_dir, jnp.int32)])
    rates = decay * (-LOG2E)
    owner_rates = lax.dynamic_slice(
        rates, (owner_dir, owner_group * owner_states, owner_tile * tile), (1, owner_states, tile)
    )[0]

    piece = 2 * LANES
    sent = pl.pallas_call(
        pack_kernel,
        out_shape=pltpu.VMEM((SUB * rows, piece), bf16),
        compiler_params=limits(3),
        name="pack",
    )(in_hbm(tile_embed), in_hbm(destination[None, :]))
    arrived = lax.all_to_all(
        sent.reshape(rows, SUB, piece), AXES, split_axis=0, concat_axis=0, tiled=True
    ).reshape(SUB * rows, piece)
    gate = jax.nn.silu(jnp.dot(tile_embed, w_gate, preferred_element_type=f32))

    plain, first_out, second_out = on_chip(
        edges_kernel,
        "edges",
        3,
        (
            pltpu.VMEM((rows, model + piece), bf16),
            pltpu.VMEM((SUB, model), bf16),
            pltpu.VMEM((SUB, model), bf16),
        ),
        arrived,
    )
    pairs = [(i, i + 1) for i in range(0, shards, 2)]
    first_in = lax.ppermute(first_out, AXES, pairs + [(j, i) for i, j in pairs])
    pairs = [(i, i + 1) for i in range(1, shards - 1, 2)]
    second_in = lax.ppermute(second_out, AXES, pairs + [(j, i) for i, j in pairs])
    hbm_spec = pl.BlockSpec(memory_space=pltpu.HBM)
    vmem_spec = pl.BlockSpec(memory_space=pltpu.VMEM)
    weights = (w_inner, x_project, dt_project)
    edge = SUB * (taps - 1)
    results = (
        pltpu.VMEM((2, rows, width), bf16),
        pltpu.VMEM((2, rows, LANES), f32),
        pltpu.VMEM((2, edge, width), f32),
        *(pltpu.VMEM(w.shape, w.dtype) for w in weights),
        pltpu.HBM((rows, LANES), f32),
    )
    u, proj, edge_sums, w_inner, x_project, dt_project, places = pl.pallas_call(
        inner_kernel,
        out_shape=results,
        in_specs=[vmem_spec] * 3 + [hbm_spec] * 3,
        out_specs=(vmem_spec,) * (len(results) - 1) + (hbm_spec,),
        scratch_shapes=[
            pltpu.VMEM((rows, model), bf16),
            pltpu.VMEM((rows, LANES), f32),
            pltpu.VMEM((rows + 2 * edge, width // 4), f32),
            pltpu.SemaphoreType.DMA((7,)),
        ],
        compiler_params=limits(4),
        name="inner",
    )(
        *(in_vmem(operand) for operand in (plain, conv_weight, conv_bias)),
        *(in_hbm(w) for w in weights),
    )

    operands = (
        proj, edge_sums, first_in, second_in, w_inner, conv_weight, x_project, dt_project, dt_bias, rates, u,
    )
    on_chip_results = [
        pltpu.VMEM((2, rows, LANES), f32),
        pltpu.VMEM((2, rows, width), f32),
        pltpu.VMEM((2, state_groups, groups, 4, tile), bf16),
        pltpu.VMEM((2, states, SUB, width), f32),
        pltpu.VMEM((2, SUB, width), f32),
        pltpu.VMEM((2, states, rows, LANES), f32),
    ]
    u, proj, dt, payload, ends, span, _ = pl.pallas_call(
        states_kernel,
        out_shape=(
            pltpu.HBM((2, rows, width), bf16),
            pltpu.HBM((2, rows, LANES), f32),
            pltpu.HBM((2, rows, width), f32),
            pltpu.HBM((2, state_groups, groups, 4, tile), bf16),
            pltpu.HBM((2, states, SUB, width), f32),
            pltpu.HBM((2, SUB, width), f32),
            pltpu.VMEM((2, rows, width), bf16),
        ),
        in_specs=[pl.BlockSpec(memory_space=pltpu.SMEM)] + [vmem_spec] * len(operands),
        out_specs=(hbm_spec,) * 6 + (vmem_spec,),
        input_output_aliases={len(operands): 6},
        scratch_shapes=on_chip_results
        + [
            pltpu.VMEM((2 * SUB, model), bf16),
            pltpu.SemaphoreType.DMA((12,)),
        ],
        compiler_params=limits(14),
        name="block_states",
    )(flags, *(in_vmem(operand) for operand in operands))

    part = 4 * LANES
    shared = lax.all_to_all(
        payload.reshape(shards, 4, tile), AXES, split_axis=0, concat_axis=0, tiled=True
    )
    entry = pl.pallas_call(
        entry_kernel,
        out_shape=pltpu.HBM((2, states, SUB, width), f32),
        grid=(width // part,),
        in_specs=[
            pl.BlockSpec((2, states, SUB, part), lambda i: (0, 0, 0, i)),
            pl.BlockSpec((2, SUB, part), lambda i: (0, 0, i)),
            pl.BlockSpec((2, states, part), lambda i: (0, 0, i)),
        ],
        out_specs=pl.BlockSpec((2, states, SUB, part), lambda i: (0, 0, 0, i)),
        compiler_params=limits(3),
        name="entries",
    )(in_hbm(ends), in_hbm(span), rates)
    shared, entry = lax.optimization_barrier((shared, entry))
    entering = on_chip(
        relay_kernel,
        "relay",
        2,
        pltpu.VMEM((shards, owner_states, tile), bf16),
        keep, shared, owner_rates,
        scalars=1,
    )
    entering = lax.all_to_all(entering, AXES, split_axis=0, concat_axis=0, tiled=True)
    entering = entering.reshape(2, state_groups, groups, owner_states, tile)

    totals = pl.pallas_call(
        outputs_kernel,
        out_shape=pltpu.HBM((SUB * rows, tile), bf16),
        grid=(width // part,),
        in_specs=[
            vmem_spec,
            pl.BlockSpec((2, states, SUB, part), lambda i: (0, 0, 0, i)),
            pl.BlockSpec((2, rows, part), lambda i: (0, 0, i)),
            pl.BlockSpec((2, rows, part), lambda i: (0, 0, i)),
            pl.BlockSpec((2, rows, LANES), lambda i: (0, 0, 0)),
            pl.BlockSpec((2, states, part), lambda i: (0, 0, i)),
            pl.BlockSpec((2, part), lambda i: (0, i)),
            pl.BlockSpec((rows, LANES), lambda i: (0, 0)),
        ],
        out_specs=pl.BlockSpec((SUB * rows, tile), lambda i: (0, 0)),
        scratch_shapes=[
            pltpu.VMEM((2, slots // 2, 2 * PACK, PACK * states), bf16),
            pltpu.VMEM((2, states, rows, LANES), f32),
            pltpu.VMEM((rows, width), bf16),
        ],
        compiler_params=limits(12),
        name="block_outputs",
    )(
        in_vmem(entering),
        *(in_hbm(array) for array in (entry, dt, u, proj)),
        rates,
        skip_gain,
        in_hbm(places),
    )

    returned = lax.all_to_all(
        totals.reshape(rows, SUB, tile), AXES, split_axis=0, concat_axis=0, tiled=True
    ).reshape(SUB * rows, tile)
    return pl.pallas_call(
        gate_kernel,
        out_shape=jax.ShapeDtypeStruct((rows, width), bf16),
        compiler_params=limits(5),
        name="gated",
    )(in_vmem(returned), gate)


def solution(mesh):
    placed = (P(AXES, None), P(AXES)) + (P(),) * 10
    return jax.shard_map(
        local, mesh=mesh, in_specs=placed, out_specs=P(AXES, None), check_vma=False
    )
```

```python
import functools

import jax
import jax.numpy as jnp
from jax import lax
from jax.experimental import pallas as pl
from jax.experimental.pallas import tpu as pltpu
from jax.sharding import PartitionSpec as P

AXES = ("seq", "slide")
SUB = 8
LANES = 128
PACK = 16
LOG2E = 1.4426950408889634


def spread_index(rows, turned=False):
    shape = (rows, rows)
    row = lax.broadcasted_iota(jnp.int32, shape, 1 if turned else 0)
    col = lax.broadcasted_iota(jnp.int32, shape, 0 if turned else 1)
    group = rows // SUB
    hit = (row // SUB == col % group) & (row % SUB == col // group)
    return hit.astype(jnp.float32).astype(jnp.bfloat16)


def as_bf16(product):
    return product.astype(jnp.bfloat16)


def matmul(left, right):
    return jnp.dot(left, right, preferred_element_type=jnp.float32)


def over_rows(left, right):
    return lax.dot_general(
        left, right, (((0,), (0,)), ((), ())), preferred_element_type=jnp.float32
    )


def chunked(pieces, out):
    rows = pieces[0].shape[0]
    group = rows // SUB
    spread = spread_index(rows)
    blank = [jnp.zeros_like(pieces[0])] * (SUB - len(pieces))
    for q in range(SUB):
        part = [piece[group * q : group * q + group] for piece in list(pieces) + blank]
        out[rows * q : rows * q + rows] = as_bf16(matmul(spread, jnp.concatenate(part, axis=0)))


def pack_kernel(embed, destination, out):
    rows = embed.shape[0]
    width = out.shape[1]
    pieces = [embed[:, at : at + width] for at in range(0, embed.shape[1], width)]
    row = lax.broadcasted_iota(jnp.int32, (rows, rows), 0)
    col = lax.broadcasted_iota(jnp.int32, (rows, rows), 1)
    offset = jnp.where(row == col, destination[...] - rows * col, 0)
    offset = as_bf16(offset.astype(jnp.float32))
    pieces.append(as_bf16(matmul(offset, jnp.ones((rows, width), jnp.bfloat16))))
    chunked(pieces, out)


def row_positions(shape, per_sub):
    lane = lax.broadcasted_iota(jnp.int32, shape, 1)
    return (lane % SUB) * per_sub + lane // SUB


def one_hot(pos):
    place = row_positions(pos.shape, pos.shape[1] // SUB)
    hit = pos.astype(jnp.int32) == place
    return hit.astype(jnp.float32).astype(jnp.bfloat16)


def edges_kernel(arrived, plain, first_out, second_out):
    rows = plain.shape[0]
    group = rows // SUB
    width = arrived.shape[1]
    pieces = plain.shape[1] // width
    gather = spread_index(rows, turned=True)
    for q in range(SUB):
        part = as_bf16(matmul(gather, arrived[rows * q : rows * q + rows]))
        for k in range(pieces):
            plain[group * q : group * q + group, width * k : width * k + width] = part[
                group * k : group * k + group
            ]
    model = width * (pieces - 1)
    pos = plain[:, model : model + LANES].astype(jnp.float32)
    lane = lax.broadcasted_iota(jnp.int32, pos.shape, 1)
    ahead = lane + rows - 3
    behind = lane % SUB
    odd = lax.axis_index(AXES[1]) % 2
    early = lane < SUB
    edge = jnp.where(early == (odd == 0), jnp.where(early, ahead, ahead - SUB), behind)
    edge = jnp.where((lane % SUB < 3) & (lane < 2 * SUB), edge, -1)
    hit = (pos.astype(jnp.int32) == edge).astype(jnp.float32).astype(jnp.bfloat16)
    ends = as_bf16(over_rows(hit, plain[:, :model]))
    first_out[...] = ends[:SUB]
    second_out[...] = ends[SUB : 2 * SUB]


def inner_kernel(
    plain,
    conv_weight,
    conv_bias,
    weight,
    x_project,
    dt_project,
    u_out,
    proj_out,
    edge_sums,
    weight_here,
    x_here,
    dt_here,
    places_result,
    rows_in,
    places,
    extended,
    sems,
):
    parts = sems.shape[0] - 3
    width = weight.shape[1] // parts
    rows, model = rows_in.shape
    taps = conv_weight.shape[1]
    reach = taps - 1
    slots = rows // SUB
    moves = []
    for k in range(parts):
        cols = pl.ds(k * width, width)
        moves.append((weight.at[:, cols], weight_here.at[:, cols]))
        if k == 0:
            moves.append((x_project, x_here))
    moves.append((dt_project, dt_here))
    copies = [
        pltpu.make_async_copy(here, there, sems.at[k]) for k, (here, there) in enumerate(moves)
    ]
    for copy in copies:
        copy.start()
    pos = plain[:, model : model + LANES].astype(jnp.float32)
    places[...] = pos
    copies.append(pltpu.make_async_copy(places, places_result, sems.at[parts + 2]))
    copies[-1].start()
    rows_in[...] = as_bf16(over_rows(one_hot(pos), plain[:, :model]))
    proj_out[...] = jnp.zeros_like(proj_out)
    row = sublane((SUB, width))
    for k in range(parts):
        cols = slice(k * width, k * width + width)
        if k == 0:
            copies[0].wait()
            copies[1].wait()
        else:
            copies[k + 1].wait()
        main = as_bf16(matmul(rows_in[...], weight_here[:, cols])).astype(jnp.float32)
        extended[SUB * reach : SUB * reach + rows] = main
        for i in range(reach):
            own = main[rows - SUB * (reach - i) : rows - SUB * (reach - i - 1)]
            extended[SUB * i : SUB * i + SUB] = jnp.where(row == 0, 0.0, pltpu.roll(own, 1, 0))
            own = main[SUB * i : SUB * i + SUB]
            base = SUB * (reach + slots + i)
            extended[base : base + SUB] = jnp.where(
                row == SUB - 1, 0.0, pltpu.roll(own, SUB - 1, 0)
            )
        for d in range(2):
            mixed = conv_bias[d : d + 1, cols]
            for tap in range(taps):
                base = SUB * (2 * reach - tap if d else tap)
                mixed = mixed + conv_weight[d, tap : tap + 1, cols] * extended[base : base + rows]
            edge = SUB * reach
            edge_sums[d, :, cols] = mixed[rows - edge :] if d else mixed[:edge]
            u = as_bf16(silu(mixed))
            u_out[d, :, cols] = u
            proj_out[d] += matmul(u, x_here[d, cols, :])
    copies[parts + 1].wait()
    copies[parts + 2].wait()


def sublane(shape):
    return lax.broadcasted_iota(jnp.int32, shape, 0)


def shift_sublanes(tile, count, reverse):
    return pltpu.roll(tile, SUB - count if reverse else count, 0)


def in_reach(count, reverse):
    row = sublane((SUB, LANES))
    return row < SUB - count if reverse else row >= count


def outside(total, reverse):
    for count in (1, 2, 4):
        moved = shift_sublanes(total, count, reverse)
        total = total + jnp.where(in_reach(count, reverse), moved, 0.0)
    return jnp.where(in_reach(1, reverse), shift_sublanes(total, 1, reverse), 0.0)


def tiles_of(array):
    return [array[SUB * t : SUB * t + SUB] for t in range(array.shape[0] // SUB)]


def in_order(count, reverse):
    return list(range(count))[::-1] if reverse else list(range(count))


def spread_columns(target, columns, first, count):
    row = lax.broadcasted_iota(jnp.int32, (2 * count, count * LANES), 0)
    at = lax.broadcasted_iota(jnp.int32, (2 * count, count * LANES), 1)
    repeat = (row % count == at // LANES).astype(jnp.float32).astype(jnp.bfloat16)
    parts = [part[:, first : first + count] for part in halves(columns)]
    wide = matmul(jnp.concatenate(parts, axis=1), repeat)
    for n in range(count):
        target[n] = wide[:, LANES * n : LANES * n + LANES]


def silu(v):
    half = 0.5 * v
    return half + half * jnp.tanh(half)


def halves(array):
    high = as_bf16(array)
    return high, as_bf16(array - high.astype(jnp.float32))


def paired(first, second):
    return as_bf16(jnp.concatenate([first, second], axis=0))


def sum_over_states(columns, first, states):
    rows = columns.shape[0]
    size = (columns.shape[1], PACK * states)
    col = lax.broadcasted_iota(jnp.int32, size, 0)
    at = lax.broadcasted_iota(jnp.int32, size, 1)
    repeat = (col == first + at // PACK).astype(jnp.float32).astype(jnp.bfloat16)
    size = (rows, PACK * states)
    row = lax.broadcasted_iota(jnp.int32, size, 0)
    at = lax.broadcasted_iota(jnp.int32, size, 1)
    own = row % PACK == at % PACK
    return [as_bf16(jnp.where(own, matmul(part, repeat), 0.0)) for part in halves(columns)]


def softplus(v):
    return jnp.maximum(v, 0.0) + jnp.log(1.0 + jnp.exp(-jnp.abs(v)))


def states_kernel(
    flags,
    proj_in,
    edge_sums,
    first_in,
    second_in,
    w_inner,
    conv_weight,
    x_project,
    dt_project,
    dt_bias,
    rates,
    u_in,
    u_result,
    proj_result,
    dt_result,
    payload_result,
    ends_result,
    span_result,
    u_out,
    proj_out,
    dt_out,
    payload,
    ends,
    span,
    b_wide,
    edge_rows,
    sems,
):
    copies = [
        pltpu.make_async_copy(here, there, sems.at[k])
        for k, (here, there) in enumerate(
            (
                (u_out, u_result),
                (proj_out, proj_result),
                (dt_out, dt_result),
                (payload.at[0], payload_result.at[0]),
                (payload.at[1], payload_result.at[1]),
            )
        )
    ]
    _, rows, channels = u_out.shape
    taps = conv_weight.shape[1]
    reach = taps - 1
    width = channels // 4
    states = rates.shape[1]
    rank = dt_project.shape[1]
    slots = rows // SUB
    tile = payload.shape[4]
    edge = SUB * reach
    even = flags[2] == 0
    edge_rows[:SUB] = jnp.where(even, second_in[...], first_in[...])
    edge_rows[SUB:] = jnp.where(even, first_in[...], second_in[...])
    row = sublane((SUB, width))
    projected = [jnp.zeros((edge, LANES), jnp.float32)] * 2
    inside = [slice(edge, rows), slice(0, rows - edge)]
    outermost = [slice(0, edge), slice(rows - edge, rows)]
    low = [as_bf16(proj_in[d, inside[d]][:, :rank]) for d in range(2)]
    for step in range(channels // width):
        cols = slice(step * width, step * width + width)
        for d in range(2):
            raw = matmul(low[d], dt_project[d, :, cols])
            dt_out[d, inside[d], cols] = softplus(raw + dt_bias[d : d + 1, cols])
        edges = as_bf16(matmul(edge_rows[...], w_inner[:, cols])).astype(jnp.float32)
        prior = edges[:SUB] * flags[0].astype(jnp.float32)
        later = edges[SUB:] * flags[1].astype(jnp.float32)
        for d in range(2):
            tiles = []
            for m in range(reach):
                if d:
                    terms = [(tap, later[m - tap : m - tap + 1]) for tap in range(m + 1)]
                else:
                    terms = [(tap, prior[m + tap : m + tap + 1]) for tap in range(reach - m)]
                extra = sum(conv_weight[d, tap : tap + 1, cols] * term for tap, term in terms)
                mixed = edge_sums[d, SUB * m : SUB * m + SUB, cols]
                tiles.append(mixed + jnp.where(row == (SUB - 1 if d else 0), extra, 0.0))
            u = as_bf16(silu(jnp.concatenate(tiles, axis=0)))
            first = rows - edge if d else 0
            u_out[d, first : first + edge, cols] = u
            projected[d] = projected[d] + matmul(u, x_project[d, cols, :])
    copies[0].start()
    for d in range(2):
        proj_out[d] = proj_in[d]
        first = rows - edge if d else 0
        proj_out[d, first : first + edge] = projected[d]
    copies[1].start()
    for d in range(2):
        spread_columns(b_wide.at[d], proj_out[d], rank, states)

    for d in range(2):
        low = as_bf16(projected[d][:, :rank])
        raw = matmul(low, dt_project[d])
        dt_out[d, outermost[d]] = softplus(raw + dt_bias[d : d + 1])
    copies[2].start()
    row = sublane((SUB, LANES))

    def state_block(block, carry, d):
        here = pl.ds(pl.multiple_of(block * LANES, LANES), LANES)
        group = block // (tile // LANES)
        within = pl.multiple_of((block - group * (tile // LANES)) * LANES, LANES)
        reverse = d == 1
        dt = dt_out[d, :, here]
        fed = tiles_of(dt * u_out[d, :, here].astype(jnp.float32))
        dt = tiles_of(dt)
        total = dt[0]
        for t in range(1, slots):
            total = total + dt[t]
        span[d, :, here] = total
        after_it = outside(total, not reverse)
        finals = []
        for n in range(states):
            rate = rates[d, n : n + 1, here]
            state = None
            for t in in_order(slots, reverse):
                new = fed[t] * b_wide[d, n, SUB * t : SUB * t + SUB]
                if state is not None:
                    new = jnp.exp2(dt[t] * rate) * state + new
                state = new
            ends[d, n, :, here] = state
            state = jnp.exp2(after_it * rate) * state
            finals.append(jnp.sum(state, axis=0, keepdims=True))
        whole = jnp.sum(total, axis=0, keepdims=True)
        for n in range(0, states, 2):
            out = jnp.where(row == 0, finals[n], finals[n + 1])
            out = jnp.where(row >= 2, whole, out)
            payload[d, n // 2, group, :, pl.ds(within, LANES)] = as_bf16(out[:4])
        return carry

    thirds = channels // LANES // 3
    for d in range(2):
        for part in range(3):
            body = functools.partial(state_block, d=d)
            lax.fori_loop(part * thirds, part * thirds + thirds, body, 0)
            cols = pl.ds(part * thirds * LANES, thirds * LANES)
            copies.append(
                pltpu.make_async_copy(
                    ends.at[d, :, :, cols],
                    ends_result.at[d, :, :, cols],
                    sems.at[5 + 3 * d + part],
                )
            )
            copies[-1].start()
        copies[3 + d].start()
    copies.append(pltpu.make_async_copy(span, span_result, sems.at[11]))
    copies[-1].start()
    for copy in copies:
        copy.wait()


def entry_kernel(ends, span, rates, entry):
    states = rates.shape[1]
    for at in range(0, span.shape[2], LANES):
        here = slice(at, at + LANES)
        for d in range(2):
            reverse = d == 1
            near = in_reach(1, reverse)
            for n in range(states):
                state = ends[d, n, :, here]
                keep = jnp.exp2(span[d, :, here] * rates[d, n : n + 1, here])
                for count in (1, 2, 4):
                    keep = jnp.where(in_reach(count, reverse), keep, 0.0)
                    state = state + keep * shift_sublanes(state, count, reverse)
                    if count < 4:
                        keep = keep * shift_sublanes(keep, count, reverse)
                entry[d, n, :, here] = jnp.where(near, shift_sublanes(state, 1, reverse), 0.0)


def relay_kernel(keep, payload, rates, entering):
    blocks = payload.shape[0]
    backward = keep[blocks]

    def block_step(i, state):
        at = jnp.where(backward == 1, blocks - 1 - i, i)
        state = state * keep[at].astype(jnp.float32)
        entering[at] = state.astype(jnp.bfloat16)
        row = payload[at].astype(jnp.float32)
        return jnp.exp2(rates[...] * row[2:3]) * state + row[0:2]

    lax.fori_loop(0, blocks, block_step, jnp.zeros(rates.shape, jnp.float32), unroll=16)


def outputs_kernel(
    entering,
    entry,
    dt_in,
    u_in,
    proj,
    rates,
    skip_gain,
    places,
    out,
    left,
    b_wide,
    placed,
):
    step = pl.program_id(0)
    states = rates.shape[1]
    _, rows, channels = dt_in.shape
    slots = rows // SUB
    rank = proj.shape[2] - 2 * states
    tile = entering.shape[4]

    @pl.when(step == 0)
    def _():
        for d in range(2):
            spread_columns(b_wide.at[d], proj[d], rank, states)
            parts = sum_over_states(proj[d], rank + states, states)
            for k in range(slots // 2):
                for i, part in enumerate(parts):
                    left[d, k, PACK * i : PACK * i + PACK] = part[PACK * k : PACK * k + PACK]

    def swept(at, d):
        here = slice(at * LANES, at * LANES + LANES)
        block = step * (channels // LANES) + at
        group = block // (tile // LANES)
        within = pl.multiple_of((block - group * (tile // LANES)) * LANES, LANES)
        reverse = d == 1
        total = dt_in[d, :SUB, here]
        for t in range(1, slots):
            total = total + dt_in[d, SUB * t : SUB * t + SUB, here]
        ahead = outside(total, reverse)
        state = []
        for n in range(states):
            pair = entering[d, n // 2, group, :, pl.ds(within, LANES)].astype(jnp.float32)
            carried = jnp.exp2(ahead * rates[d, n : n + 1, here]) * pair[n % 2 : n % 2 + 1]
            state.append(carried + entry[d, n, :, here])
        sums = [None] * (slots // 2)
        for k in in_order(slots // 2, reverse):
            right = []
            two = slice(PACK * k, PACK * k + PACK)
            u = u_in[d, two, here].astype(jnp.float32)
            dt = dt_in[d, two, here]
            fed = tiles_of(dt * u)
            dt = tiles_of(dt)
            for n in range(states):
                rate = rates[d, n : n + 1, here]
                both = []
                for t in in_order(2, reverse):
                    first = PACK * k + SUB * t
                    new = fed[t] * b_wide[d, n, first : first + SUB]
                    state[n] = jnp.exp2(dt[t] * rate) * state[n] + new
                    both.append(state[n])
                right.append(paired(*(both[::-1] if reverse else both)))
            part = matmul(left[d, k], jnp.concatenate(right, axis=0))
            sums[k] = part[:PACK] + part[PACK:] + skip_gain[d : d + 1, here] * u
        return jnp.concatenate(sums, axis=0)

    pick = one_hot(places[...])
    for at in range(channels // LANES):
        total = swept(at, 0) + swept(at, 1)
        start = pl.multiple_of(step * channels + at * LANES, LANES)
        placed[:, pl.ds(start, LANES)] = as_bf16(matmul(pick, as_bf16(total)))

    @pl.when(step == pl.num_programs(0) - 1)
    def _():
        chunked([placed[:, tile * k : tile * k + tile] for k in range(SUB)], out)


def gate_kernel(returned, gate, out):
    rows = out.shape[0]
    group = rows // SUB
    width = returned.shape[1]
    gather = spread_index(rows, turned=True)
    for q in range(SUB):
        part = matmul(gather, returned[rows * q : rows * q + rows])
        here = slice(group * q, group * q + group)
        for k in range(SUB):
            cols = slice(width * k, width * k + width)
            out[here, cols] = as_bf16(part[group * k : group * k + group] * gate[here, cols])


def limits(mebibytes):
    return pltpu.CompilerParams(vmem_limit_bytes=mebibytes * 1024 * 1024)


def in_vmem(array):
    return pltpu.with_memory_space_constraint(array, pltpu.VMEM)


def in_hbm(array):
    return pltpu.with_memory_space_constraint(array, pltpu.HBM)


def on_chip(kernel, name, mebibytes, results, *operands, scalars=0, scratch=()):
    places = [pltpu.SMEM] * scalars + [pltpu.VMEM] * (len(operands) - scalars)
    one = pl.BlockSpec(memory_space=pltpu.VMEM)
    return pl.pallas_call(
        kernel,
        out_shape=results,
        in_specs=[pl.BlockSpec(memory_space=place) for place in places],
        out_specs=tuple(one for _ in results) if isinstance(results, tuple) else one,
        scratch_shapes=list(scratch),
        compiler_params=limits(mebibytes),
        name=name,
    )(
        *(
            in_vmem(operand) if place is pltpu.VMEM else operand
            for operand, place in zip(operands, places)
        )
    )


def local(
    tile_embed,
    destination,
    slide_lengths,
    w_inner,
    w_gate,
    conv_weight,
    conv_bias,
    x_project,
    dt_project,
    dt_bias,
    decay,
    skip_gain,
):
    f32, bf16 = jnp.float32, jnp.bfloat16
    shards = lax.axis_size(AXES)
    me = lax.axis_index(AXES)
    rows, model = tile_embed.shape
    width = w_inner.shape[1]
    states = decay.shape[1]
    rank = dt_project.shape[1]
    taps = conv_weight.shape[1]
    tile = 3 * LANES
    groups = width // tile
    owner_states = 2 * groups * states // shards
    state_groups = states // owner_states
    slots = rows // SUB

    blocks = jnp.arange(shards, dtype=jnp.int32)
    slide = jnp.arange(slide_lengths.shape[0], dtype=jnp.int32)
    ends = jnp.sum(jnp.where(slide[:, None] <= slide[None, :], slide_lengths[:, None], 0), axis=0)
    starts = ends - slide_lengths
    opens = jnp.any(blocks[:, None] * rows == starts[None, :], axis=1)
    closes = jnp.any((blocks[:, None] + 1) * rows == ends[None, :], axis=1)
    mine = blocks == me
    flags = jnp.stack([~jnp.any(opens & mine), ~jnp.any(closes & mine), me % 2 == 1]).astype(jnp.int32)
    owner_dir = me // (state_groups * groups)
    owner_group = (me // groups) % state_groups
    owner_tile = me % groups
    keep = jnp.where(owner_dir == 1, ~closes, ~opens).astype(jnp.int32)
    keep = jnp.concatenate([keep, jnp.full((SUB,), owner_dir, jnp.int32)])
    rates = decay * (-LOG2E)
    owner_rates = lax.dynamic_slice(
        rates, (owner_dir, owner_group * owner_states, owner_tile * tile), (1, owner_states, tile)
    )[0]

    piece = 2 * LANES
    sent = pl.pallas_call(
        pack_kernel,
        out_shape=pltpu.VMEM((SUB * rows, piece), bf16),
        compiler_params=limits(3),
        name="pack",
    )(in_hbm(tile_embed), in_hbm(destination[None, :]))
    arrived = lax.all_to_all(
        sent.reshape(rows, SUB, piece), AXES, split_axis=0, concat_axis=0, tiled=True
    ).reshape(SUB * rows, piece)
    gate = jax.nn.silu(jnp.dot(tile_embed, w_gate, preferred_element_type=f32))

    plain, first_out, second_out = on_chip(
        edges_kernel,
        "edges",
        3,
        (
            pltpu.VMEM((rows, model + piece), bf16),
            pltpu.VMEM((SUB, model), bf16),
            pltpu.VMEM((SUB, model), bf16),
        ),
        arrived,
    )
    pairs = [(i, i + 1) for i in range(0, shards, 2)]
    first_in = lax.ppermute(first_out, AXES, pairs + [(j, i) for i, j in pairs])
    pairs = [(i, i + 1) for i in range(1, shards - 1, 2)]
    second_in = lax.ppermute(second_out, AXES, pairs + [(j, i) for i, j in pairs])
    hbm_spec = pl.BlockSpec(memory_space=pltpu.HBM)
    vmem_spec = pl.BlockSpec(memory_space=pltpu.VMEM)
    weights = (w_inner, x_project, dt_project)
    edge = SUB * (taps - 1)
    results = (
        pltpu.VMEM((2, rows, width), bf16),
        pltpu.VMEM((2, rows, LANES), f32),
        pltpu.VMEM((2, edge, width), f32),
        *(pltpu.VMEM(w.shape, w.dtype) for w in weights),
        pltpu.HBM((rows, LANES), f32),
    )
    u, proj, edge_sums, w_inner, x_project, dt_project, places = pl.pallas_call(
        inner_kernel,
        out_shape=results,
        in_specs=[vmem_spec] * 3 + [hbm_spec] * 3,
        out_specs=(vmem_spec,) * (len(results) - 1) + (hbm_spec,),
        scratch_shapes=[
            pltpu.VMEM((rows, model), bf16),
            pltpu.VMEM((rows, LANES), f32),
            pltpu.VMEM((rows + 2 * edge, width // 4), f32),
            pltpu.SemaphoreType.DMA((7,)),
        ],
        compiler_params=limits(4),
        name="inner",
    )(
        *(in_vmem(operand) for operand in (plain, conv_weight, conv_bias)),
        *(in_hbm(w) for w in weights),
    )

    operands = (
        proj, edge_sums, first_in, second_in, w_inner, conv_weight, x_project, dt_project, dt_bias, rates, u,
    )
    on_chip_results = [
        pltpu.VMEM((2, rows, LANES), f32),
        pltpu.VMEM((2, rows, width), f32),
        pltpu.VMEM((2, state_groups, groups, 4, tile), bf16),
        pltpu.VMEM((2, states, SUB, width), f32),
        pltpu.VMEM((2, SUB, width), f32),
        pltpu.VMEM((2, states, rows, LANES), f32),
    ]
    u, proj, dt, payload, ends, span, _ = pl.pallas_call(
        states_kernel,
        out_shape=(
            pltpu.HBM((2, rows, width), bf16),
            pltpu.HBM((2, rows, LANES), f32),
            pltpu.HBM((2, rows, width), f32),
            pltpu.HBM((2, state_groups, groups, 4, tile), bf16),
            pltpu.HBM((2, states, SUB, width), f32),
            pltpu.HBM((2, SUB, width), f32),
            pltpu.VMEM((2, rows, width), bf16),
        ),
        in_specs=[pl.BlockSpec(memory_space=pltpu.SMEM)] + [vmem_spec] * len(operands),
        out_specs=(hbm_spec,) * 6 + (vmem_spec,),
        input_output_aliases={len(operands): 6},
        scratch_shapes=on_chip_results
        + [
            pltpu.VMEM((2 * SUB, model), bf16),
            pltpu.SemaphoreType.DMA((12,)),
        ],
        compiler_params=limits(14),
        name="block_states",
    )(flags, *(in_vmem(operand) for operand in operands))

    part = 6 * LANES
    shared = lax.all_to_all(
        payload.reshape(shards, 4, tile), AXES, split_axis=0, concat_axis=0, tiled=True
    )
    entry = pl.pallas_call(
        entry_kernel,
        out_shape=pltpu.HBM((2, states, SUB, width), f32),
        grid=(width // part,),
        in_specs=[
            pl.BlockSpec((2, states, SUB, part), lambda i: (0, 0, 0, i)),
            pl.BlockSpec((2, SUB, part), lambda i: (0, 0, i)),
            pl.BlockSpec((2, states, part), lambda i: (0, 0, i)),
        ],
        out_specs=pl.BlockSpec((2, states, SUB, part), lambda i: (0, 0, 0, i)),
        compiler_params=limits(6),
        name="entries",
    )(in_hbm(ends), in_hbm(span), rates)
    shared, entry = lax.optimization_barrier((shared, entry))
    entering = on_chip(
        relay_kernel,
        "relay",
        2,
        pltpu.VMEM((shards, owner_states, tile), bf16),
        keep, shared, owner_rates,
        scalars=1,
    )
    entering = lax.all_to_all(entering, AXES, split_axis=0, concat_axis=0, tiled=True)
    entering = entering.reshape(2, state_groups, groups, owner_states, tile)

    totals = pl.pallas_call(
        outputs_kernel,
        out_shape=pltpu.HBM((SUB * rows, tile), bf16),
        grid=(width // part,),
        in_specs=[
            vmem_spec,
            pl.BlockSpec((2, states, SUB, part), lambda i: (0, 0, 0, i)),
            pl.BlockSpec((2, rows, part), lambda i: (0, 0, i)),
            pl.BlockSpec((2, rows, part), lambda i: (0, 0, i)),
            pl.BlockSpec((2, rows, LANES), lambda i: (0, 0, 0)),
            pl.BlockSpec((2, states, part), lambda i: (0, 0, i)),
            pl.BlockSpec((2, part), lambda i: (0, i)),
            pl.BlockSpec((rows, LANES), lambda i: (0, 0)),
        ],
        out_specs=pl.BlockSpec((SUB * rows, tile), lambda i: (0, 0)),
        scratch_shapes=[
            pltpu.VMEM((2, slots // 2, 2 * PACK, PACK * states), bf16),
            pltpu.VMEM((2, states, rows, LANES), f32),
            pltpu.VMEM((rows, width), bf16),
        ],
        compiler_params=limits(14),
        name="block_outputs",
    )(
        in_vmem(entering),
        *(in_hbm(array) for array in (entry, dt, u, proj)),
        rates,
        skip_gain,
        in_hbm(places),
    )

    returned = lax.all_to_all(
        totals.reshape(rows, SUB, tile), AXES, split_axis=0, concat_axis=0, tiled=True
    ).reshape(SUB * rows, tile)
    return pl.pallas_call(
        gate_kernel,
        out_shape=jax.ShapeDtypeStruct((rows, width), bf16),
        compiler_params=limits(5),
        name="gated",
    )(in_vmem(returned), gate)


def solution(mesh):
    placed = (P(AXES, None), P(AXES)) + (P(),) * 10
    return jax.shard_map(
        local, mesh=mesh, in_specs=placed, out_specs=P(AXES, None), check_vma=False
    )
```
